128 devices in a mesh: seq: 32 (over x, z, core), head: 4 (over y).
Axes of the slice: x: 4, y: 4, z: 4, core: 2. Of those that a mesh axis runs over, the one named last changes fastest.
Arguments:
- queries: bfloat16 [32768, 2048], P('seq', 'head'), may hold values from -64 to 64
- keys: bfloat16 [32768, 2048], P('seq', 'head'), may hold values from -16 to 16
- values: bfloat16 [32768, 2048], P('seq', 'head'), may hold values from -6 to 6
- span_bounds: int32 [64, 2], replicated, may hold values from 0 to 32768, as said below
- mem_decay: float32 [32, 16], P(None, 'head'), may hold values from 0.01 to 1
- mem_gate: float32 [16], P('head'), may hold values from -2 to 2
- out_weight: bfloat16 [2048, 4096], P('head'), may hold values from -0.125 to 0.125
Outputs:
- mixed: bfloat16 [32768, 4096], P('seq', 'head')
The draws below stay inside these ranges and needn't reach their ends.
Inputs may be any that keep to these rules, and one draw needn't show every extreme that they name: `span_bounds`: slot k lies in segment k // 2, inside the k % 2-th of 2 equal parts of it; start <= end, an empty slot has start == end; some slot covers a whole part.
All inputs are finite; a program needn't handle non-finite values.
Results may differ from the reference program's by a relative error of at most 0.0052.
The reference program's roundings to bfloat16 on the way (of `weights` and `attended`) count: a program that leaves them out, or rounds other values in their place, can miss the bound.
Values may be sent and summed in bfloat16 or wider, within the bound.
A program may use at most 128 MiB of HBM per device.

```python
import math
import jax
import jax.numpy as jnp
from jax import lax

D = 4096
HEAD_DIM = 128
SEG = 1024
BAND = 512
SPAN_DEV = 2
HEAD_TOTAL = 16
TOKENS = 32768
SPANS = 64
N_SEQ = 32


def query_key_pair(key):
    random_subkeys = jax.random.split(jax.random.fold_in(key, 7), 2)
    query_draw = jnp.clip(jax.random.normal(random_subkeys[0], (TOKENS, HEAD_TOTAL * HEAD_DIM), jnp.float32), -6.0, 6.0)
    key_draw = jnp.clip(jax.random.normal(random_subkeys[1], (TOKENS, HEAD_TOTAL * HEAD_DIM), jnp.float32), -6.0, 6.0)
    return (query_draw, key_draw)


def draw_queries(key, part):
    return query_key_pair(key)[0].astype(jnp.bfloat16)


def draw_keys(key, part):
    return query_key_pair(key)[1].astype(jnp.bfloat16)


def draw_span_bounds(key, part):
    random_subkeys = jax.random.split(key, 5)
    region = SEG // SPAN_DEV
    heaviness = jax.random.randint(random_subkeys[0], (N_SEQ, 1), 0, 4)
    offset = jax.random.randint(random_subkeys[1], (N_SEQ, SPAN_DEV), 0, region // 4 + 1)
    length_raw = jax.random.randint(random_subkeys[2], (N_SEQ, SPAN_DEV), region // 4, region + 1)
    length = jnp.minimum(length_raw, region - offset)
    live = (jax.random.randint(random_subkeys[3], (N_SEQ, SPAN_DEV), 0, 4) < heaviness).astype(jnp.int32)
    chosen_slot = jax.random.randint(random_subkeys[4], (), 0, N_SEQ * SPAN_DEV)
    flat_index = jnp.arange(N_SEQ * SPAN_DEV).reshape(N_SEQ, SPAN_DEV)
    forced = flat_index == chosen_slot
    offset = jnp.where(forced, 0, offset)
    length = jnp.where(forced, region, length)
    live = jnp.where(forced, 1, live)
    seg_start = (jnp.arange(N_SEQ) * SEG)[:, None]
    part_start = (jnp.arange(SPAN_DEV) * region)[None, :]
    starts = seg_start + part_start + offset
    ends = starts + length * live
    return jnp.stack([starts.reshape(-1), ends.reshape(-1)], axis=1).astype(jnp.int32)


def draw_mem_decay(key, part):
    random_subkeys = jax.random.split(key, 6)
    slow_heads = jax.random.uniform(random_subkeys[0], (HEAD_TOTAL,), jnp.float32) < 0.5
    total_loss = jnp.where(slow_heads, jax.random.uniform(random_subkeys[1], (HEAD_TOTAL,), jnp.float32, 0.3, 2.0), jax.random.uniform(random_subkeys[2], (HEAD_TOTAL,), jnp.float32, 20.0, 60.0))
    iteration_loss = total_loss[None, :] / N_SEQ * jax.random.uniform(random_subkeys[3], (N_SEQ, HEAD_TOTAL), jnp.float32, 0.5, 1.5)
    surge_events = jax.random.uniform(random_subkeys[4], (N_SEQ, HEAD_TOTAL), jnp.float32) < 3.0 / N_SEQ
    surge_loss_value = jnp.where(surge_events, -jnp.log(jax.random.uniform(random_subkeys[5], (N_SEQ, HEAD_TOTAL), jnp.float32, 0.5, 0.8)), 0.0)
    return jnp.maximum(jnp.exp(-iteration_loss - surge_loss_value), 0.01)


def levels(own_key, dims, shards, low, top_value):
    level = 1.0
    for axis_at, parts in shards:
        draws = jax.random.uniform(jax.random.fold_in(jax.random.fold_in(own_key, 6), axis_at), (parts,), jnp.float32, low / len(shards), top_value / len(shards))
        level = level * jnp.repeat(jnp.exp(draws), dims[axis_at] // parts).reshape((-1,) + (1,) * (len(dims) - 1 - axis_at))
    return level


def centred(rng, dims, deviation, bound, shards=(), dtype=jnp.bfloat16):
    result = deviation * jax.random.normal(rng, dims, jnp.float32)
    if shards:
        result = result * levels(rng, dims, shards, -0.22, 0.18)
    return jnp.clip(result, -bound, bound).astype(dtype)


def setup_inputs(seed: int = 0) -> dict:
    arg_keys = jax.random.split(jax.random.key(seed), 8)
    return {
        "queries": draw_queries(jax.random.fold_in(arg_keys[7], 71), 0),
        "keys": draw_keys(jax.random.fold_in(arg_keys[7], 71), 0),
        "values": centred(arg_keys[2], (TOKENS, HEAD_TOTAL * HEAD_DIM), 1.0, 6.0, ((0, 32), (1, 4))),
        "span_bounds": draw_span_bounds(jax.random.fold_in(arg_keys[7], 71), 0),
        "mem_decay": draw_mem_decay(jax.random.fold_in(arg_keys[7], 71), 0),
        "mem_gate": jnp.clip(jax.random.uniform(arg_keys[5], (HEAD_TOTAL,), jnp.float32, -2.0, 2.0) * levels(arg_keys[5], (HEAD_TOTAL,), ((0, 4),), -0.4, 0.0), -2.0, 2.0),
        "out_weight": centred(arg_keys[6], (HEAD_TOTAL * HEAD_DIM, D), (HEAD_TOTAL * HEAD_DIM) ** -0.5, 0.125, ((0, 4),)),
    }


HIGHEST_PRECISION = lax.Precision.HIGHEST

def feature_map(values_in):
    return jnp.where(values_in > 0, values_in + 1.0, jnp.exp(jnp.minimum(values_in, 0.0)))

def local_attention(queries_3d, band_keys, band_values, query_labels, key_labels, shard_index, band_width):
    seg_rows, head_count, head_width = queries_3d.shape
    block_rows = min(seg_rows, 512)
    key_count = band_keys.shape[0]
    key_pos = jnp.arange(key_count).astype(jnp.int32) - band_width
    key_valid = (key_pos >= 0) | (shard_index > 0)
    score_scale = 1.0 / math.sqrt(head_width)
    keys_wide = band_keys.astype(jnp.float32)
    values_wide = band_values.astype(jnp.float32)

    def attend_block(block_index):
        row_start = (block_index * block_rows).astype(jnp.int32)
        query_block = lax.dynamic_slice_in_dim(queries_3d, row_start, block_rows, 0).astype(jnp.float32)
        label_block = lax.dynamic_slice_in_dim(query_labels, row_start, block_rows, 0)
        query_pos = row_start + jnp.arange(block_rows).astype(jnp.int32)
        scores = jnp.einsum('qhd,khd->hqk', query_block, keys_wide) * score_scale
        nearby = (key_pos[None, :] <= query_pos[:, None]) & (key_pos[None, :] > query_pos[:, None] - band_width) & key_valid[None, :]
        same_span = (label_block[:, None] > 0) & (label_block[:, None] == key_labels[None, :])
        visible = nearby | same_span
        scores = jnp.where(visible[None], scores, -1e+30)
        top_score = lax.optimization_barrier(jnp.max(scores, axis=-1, keepdims=True))
        weights = jnp.exp(scores - top_score)
        totals = lax.optimization_barrier(jnp.sum(weights, axis=-1))
        rounded = lax.optimization_barrier(weights.astype(jnp.bfloat16)).astype(jnp.float32)
        mixed_out = jnp.einsum('hqk,khd->qhd', rounded, values_wide)
        return mixed_out / jnp.transpose(totals)[:, :, None]
    blocks = lax.map(attend_block, jnp.arange(seg_rows // block_rows).astype(jnp.int32))
    return blocks.reshape(seg_rows, head_count, head_width)

def reference(queries, keys, values, span_bounds, mem_decay, mem_gate, out_weight):
    positions = jnp.arange(TOKENS).astype(jnp.int32)
    inside = (positions[:, None] >= span_bounds[None, :, 0]) & (positions[:, None] < span_bounds[None, :, 1])
    slot_ids = (jnp.arange(SPANS).astype(jnp.int32) + 1)[None, :]
    labels = lax.optimization_barrier(jnp.sum(inside.astype(jnp.int32) * slot_ids, axis=1)).astype(jnp.int32)
    query_seg = queries.reshape(N_SEQ, SEG, HEAD_TOTAL, HEAD_DIM)
    key_seg = keys.reshape(N_SEQ, SEG, HEAD_TOTAL, HEAD_DIM)
    value_seg = values.reshape(N_SEQ, SEG, HEAD_TOTAL, HEAD_DIM)
    label_segment = labels.reshape(N_SEQ, SEG)

    def memory_step(carry, inputs):
        memory, feat_total = carry
        shard_q, shard_k, shard_v, decay = inputs
        query_feats = feature_map(shard_q.astype(jnp.float32))
        key_feats = feature_map(shard_k.astype(jnp.float32))
        value_rows = shard_v.astype(jnp.float32)
        numer = jnp.einsum('thd,hde->the', query_feats, memory, precision=HIGHEST_PRECISION)
        denom = jnp.einsum('thd,hd->th', query_feats, feat_total, precision=HIGHEST_PRECISION) + 1.0
        readout = numer / denom[:, :, None]
        state = jnp.einsum('thd,the->hde', key_feats, value_rows, precision=HIGHEST_PRECISION)
        memory = decay[:, None, None] * memory + state
        feat_total = decay[:, None] * feat_total + lax.optimization_barrier(jnp.sum(key_feats, axis=0))
        return ((memory, feat_total), readout)
    start_memory = jnp.zeros((HEAD_TOTAL, HEAD_DIM, HEAD_DIM), jnp.float32)
    start_total = jnp.zeros((HEAD_TOTAL, HEAD_DIM), jnp.float32)
    unused, readouts = lax.scan(memory_step, (start_memory, start_total), (query_seg, key_seg, value_seg, mem_decay))

    def shard_attention(shard_index):
        earlier = jnp.maximum(shard_index - 1, 0)
        band_keys = jnp.concatenate([key_seg[earlier][SEG - BAND:], key_seg[shard_index]], axis=0)
        band_values = jnp.concatenate([value_seg[earlier][SEG - BAND:], value_seg[shard_index]], axis=0)
        query_labels = label_segment[shard_index]
        key_labels = jnp.concatenate([jnp.zeros((BAND,), jnp.int32), query_labels])
        return local_attention(query_seg[shard_index], band_keys, band_values, query_labels, key_labels, shard_index, BAND)
    local = lax.map(shard_attention, jnp.arange(N_SEQ).astype(jnp.int32))
    gate = jax.nn.sigmoid(mem_gate)[None, None, :, None]
    attended = (gate * readouts + (1.0 - gate) * local).astype(jnp.bfloat16).reshape(TOKENS, HEAD_TOTAL * HEAD_DIM)
    return jnp.dot(attended, out_weight, preferred_element_type=jnp.float32).astype(jnp.bfloat16)
```

```python
import math

import jax
import jax.numpy as jnp
from jax import lax
from jax.experimental import pallas as pl
from jax.experimental.pallas import tpu as pltpu
from jax.sharding import PartitionSpec as P

SEG = 1024
BAND = 512
PART = 512
BLOCK = 256
HALF = 128
HEADS = 4
WIDTH = 128
COLS = 1024
GROUP = 4
ROW = 8
SLICE = 72
MESH = pl.DeviceIdType.MESH
EXPONENT = math.log2(math.e) / math.sqrt(WIDTH)
F32 = jnp.float32
BF16 = jnp.bfloat16


def feature_map(values_in):
    return jnp.where(values_in > 0, values_in + 1.0, jnp.exp(jnp.minimum(values_in, 0.0)))


def two_terms(values_in):
    high = values_in.astype(BF16)
    return high, (values_in - high.astype(F32)).astype(BF16)


def dot_last(a, b):
    return lax.dot_general(a, b, (((1,), (1,)), ((), ())), preferred_element_type=F32)


def dot_first(a, b):
    return lax.dot_general(a, b, (((0,), (0,)), ((), ())), preferred_element_type=F32)


def head_columns(head):
    return pl.ds(pl.multiple_of(head * WIDTH, WIDTH), WIDTH)


def kernel(
    spans, decay, gate, q_hbm, k_hbm, v_hbm, w_hbm, out_hbm,
    kbuf, vbuf, qbuf, gbuf, wbuf, obuf, local, bias, mem_high, mem_low,
    slices_out, slices_in, total_out, totals_in, mem_out, mem_in,
    load_sem, store_sem, band_s, band_r, wy_s, wy_r, wx_s, wx_r, wc_s, wc_r,
    a_s, a_r, b_s, b_r, c_s, c_r, g_s, g_r,
):
    seq = lax.axis_index("seq")
    head = lax.axis_index("head")
    x, place = seq // ROW, seq % ROW
    core, z = seq % 2, (seq % ROW) // 2
    n_seq = GROUP * ROW

    def along_y(d):
        return (seq, (head + d) % GROUP)

    def along_x(d):
        return (((x + d) % GROUP) * ROW + place, head)

    def along_row(d):
        return (x * ROW + (place + d) % ROW, head)

    partner = (seq + 1 - 2 * core, head)
    following, previous = ((seq + 1) % n_seq, head), ((seq + n_seq - 1) % n_seq, head)
    sent = []

    def remote(src, dst, send_sem, recv_sem, device):
        return pltpu.make_async_remote_copy(
            src_ref=src, dst_ref=dst, send_sem=send_sem, recv_sem=recv_sem,
            device_id=device, device_id_type=MESH,
        )

    def send(src, dst, send_sem, recv_sem, device):
        copy = remote(src, dst, send_sem, recv_sem, device)
        copy.start()
        sent.append(copy)

    def arrived(dst, send_sem, recv_sem, device):
        remote(dst, dst, send_sem, recv_sem, device).wait_recv()

    loads = [
        pltpu.make_async_copy(k_hbm, kbuf.at[pl.ds(BAND, SEG)], load_sem.at[0]),
        pltpu.make_async_copy(v_hbm, vbuf.at[pl.ds(BAND, SEG)], load_sem.at[1]),
        pltpu.make_async_copy(q_hbm, qbuf, load_sem.at[2]),
        pltpu.make_async_copy(
            w_hbm.at[:, pl.ds(pl.multiple_of(head * COLS, COLS), COLS)], wbuf.at[0], load_sem.at[3]
        ),
    ]
    for copy in loads:
        copy.start()

    barrier = pltpu.get_barrier_semaphore()
    sources = [along_y(d) for d in range(1, GROUP)] + [along_x(d) for d in range(1, GROUP)]
    sources += [along_row(d) for d in range(1, ROW)] + [previous]
    for device in sources:
        pl.semaphore_signal(barrier, inc=1, device_id=device, device_id_type=MESH)
    pl.semaphore_wait(barrier, len(sources))

    def piece_rows(d, of_core):
        return pl.ds(pl.multiple_of((((x + GROUP - d) % GROUP) * 2 + of_core) * 64, 64), 64)

    own_rows = piece_rows(0, core)
    for d in range(1, GROUP):
        send(
            w_hbm.at[own_rows, pl.ds(pl.multiple_of(((head + d) % GROUP) * COLS, COLS), COLS)],
            wbuf.at[GROUP - d, own_rows], wy_s.at[d], wy_r.at[d], along_y(d),
        )

    def band_pieces(which):
        for n in which:
            src, dst = (k_hbm, kbuf) if n < 4 else (v_hbm, vbuf)
            rows = (n % 4) * 128
            send(
                src.at[pl.ds(SEG - BAND + rows, 128)], dst.at[pl.ds(rows, 128)],
                band_s.at[n], band_r.at[n], following,
            )

    def band_arrived():
        for n in range(8):
            dst = kbuf if n < 4 else vbuf
            arrived(dst.at[pl.ds((n % 4) * 128, 128)], band_s.at[n], band_r.at[n], previous)

    band_pieces((0, 1))
    loads[0].wait()
    loads[1].wait()

    def state_of(h, carry):
        cols = head_columns(h)
        total = jnp.zeros((WIDTH, 2 * WIDTH), F32)
        sums = jnp.zeros((8, WIDTH), F32)
        for t in range(SEG // BLOCK):
            rows = pl.ds(BAND + t * BLOCK, BLOCK)
            feats = feature_map(kbuf[rows, cols].astype(F32))
            total += dot_first(vbuf[rows, cols], jnp.concatenate(two_terms(feats), axis=1))
            sums += jnp.sum(feats.reshape(BLOCK // 8, 8, WIDTH), axis=0)
        state = total[:, :WIDTH] + total[:, WIDTH:]
        sums = jnp.broadcast_to(jnp.sum(sums, axis=0, keepdims=True), (8, WIDTH))
        for half in range(2):
            slices_out[2 * h + half, :64] = state[64 * half : 64 * half + 64]
            slices_out[2 * h + half, 64:] = sums
        return carry

    lax.fori_loop(0, HEADS, state_of, 0)

    for d in range(1, ROW):
        send(
            slices_out.at[(place + d) % ROW], slices_in.at[place], a_s.at[d], a_r.at[d], along_row(d)
        )
    slices_in[place] = slices_out[place]
    band_pieces((2, 3, 4))
    loads[2].wait()

    def attend(part, sub):
        row = part * PART + sub * BLOCK
        count = 2 * PART - sub * BLOCK
        first = spans[0, 2 * seq + part] - seq * SEG
        last = spans[1, 2 * seq + part] - seq * SEG
        r = lax.broadcasted_iota(jnp.int32, (BLOCK, count), 0)
        j = lax.broadcasted_iota(jnp.int32, (BLOCK, count), 1)
        near = (j <= r + BAND) & (j > r)
        key_at, query_at = j + (row - BAND), r + row
        if part == 0:
            near = near & (key_at >= jnp.where(seq > 0, -BAND, 0))
        same = (query_at >= first) & (query_at < last) & (key_at >= first) & (key_at < last)
        bias[:, :count] = jnp.where(near | same, 0.0, -1e30)

        def one_head(h, carry):
            cols = head_columns(h)
            keys = kbuf[pl.ds(row, count), cols]
            scores = dot_last(qbuf[pl.ds(row, BLOCK), cols], keys) + bias[:, :count]
            weights = jnp.exp2((scores - jnp.max(scores, axis=1, keepdims=True)) * EXPONENT)
            mixed = jnp.dot(
                weights.astype(BF16), vbuf[pl.ds(row, count), cols], preferred_element_type=F32
            )
            local[pl.ds(row, BLOCK), cols] = mixed / jnp.sum(weights, axis=1, keepdims=True)
            return carry

        lax.fori_loop(0, HEADS, one_head, 0)

    attend(1, 0)

    for d in range(1, ROW):
        arrived(slices_in.at[(place + ROW - d) % ROW], a_s.at[d], a_r.at[d], along_row(ROW - d))
    total = slices_in[0]
    for t in range(1, ROW):
        total = decay[z, x * ROW + t] * total + slices_in[t]
    total_out[...] = total
    for d in range(1, GROUP):
        send(total_out, totals_in.at[x], b_s.at[d], b_r.at[d], along_x(d))
    totals_in[x] = total

    foreign = pl.ds(1, GROUP - 1)
    for d in range(1, GROUP):
        arrived(wbuf.at[GROUP - d, own_rows], wy_s.at[d], wy_r.at[d], along_y(GROUP - d))
    for d in range(1, GROUP):
        piece = wbuf.at[foreign, own_rows]
        send(piece, piece, wx_s.at[d], wx_r.at[d], along_x(d))
    send(wbuf.at[foreign, own_rows], wbuf.at[foreign, own_rows], wc_s.at[0], wc_r.at[0], partner)

    attend(1, 1)

    for d in range(1, GROUP):
        arrived(totals_in.at[(x + GROUP - d) % GROUP], b_s.at[d], b_r.at[d], along_x(GROUP - d))
    memory = jnp.zeros((SLICE, WIDTH), F32)
    for n in range(GROUP):
        product = decay[z, n * ROW]
        for t in range(1, ROW):
            product = product * decay[z, n * ROW + t]
        memory = jnp.where(n < x, product * memory + totals_in[n], memory)
    for t in range(ROW):
        mem_out[t] = memory
        memory = decay[z, x * ROW + t] * memory + slices_in[t]
    for d in range(1, ROW):
        send(mem_out.at[(place + d) % ROW], mem_in.at[place], c_s.at[d], c_r.at[d], along_row(d))
    mem_in[place] = mem_out[place]
    band_pieces((5, 6, 7))

    for d in range(1, ROW):
        arrived(mem_in.at[(place + ROW - d) % ROW], c_s.at[d], c_r.at[d], along_row(ROW - d))

    def place_memory(h, carry):
        norm = jnp.broadcast_to(mem_in[2 * h, 64:65], (WIDTH, WIDTH))
        both = jnp.concatenate([mem_in[2 * h, :64], mem_in[2 * h + 1, :64], norm], axis=0)
        high, low = two_terms(both)
        mem_high[h] = high
        mem_low[h] = low
        return carry

    lax.fori_loop(0, HEADS, place_memory, 0)

    def finish(row):
        def one_head(h, carry):
            cols = head_columns(h)
            high, low = two_terms(feature_map(qbuf[pl.ds(row, BLOCK), cols].astype(F32)))
            both = dot_last(high, mem_high[h]) + dot_last(high, mem_low[h]) + dot_last(low, mem_high[h])
            readout = both[:, :WIDTH] / (both[:, WIDTH:] + 1.0)
            mix = 1.0 / (1.0 + jnp.exp(-jnp.full((1, WIDTH), gate[h], F32)))
            mixed = mix * readout + (1.0 - mix) * local[pl.ds(row, BLOCK), cols]
            gbuf[0, pl.ds(row, BLOCK), cols] = mixed.astype(BF16)
            return carry

        lax.fori_loop(0, HEADS, one_head, 0)

    chunk_rows = (512, 768, 0, 256)

    def half_rows(chunk, half):
        return pl.ds(chunk_rows[chunk] + half * HALF, HALF)

    def share(chunk):
        for half in (0, 1):
            rows, at = half_rows(chunk, half), chunk * 6 + half
            send(gbuf.at[0, rows], gbuf.at[3, rows], g_s.at[at], g_r.at[at], along_y(1))
            rows, at = half_rows(chunk, 1 - half), chunk * 6 + 3 - half
            send(gbuf.at[0, rows], gbuf.at[1, rows], g_s.at[at], g_r.at[at], along_y(3))

    def relay(chunk):
        rows, at = half_rows(chunk, 0), chunk * 6
        arrived(gbuf.at[3, rows], g_s.at[at], g_r.at[at], along_y(3))
        send(gbuf.at[3, rows], gbuf.at[2, rows], g_s.at[at + 4], g_r.at[at + 4], along_y(1))
        rows = half_rows(chunk, 1)
        arrived(gbuf.at[1, rows], g_s.at[at + 3], g_r.at[at + 3], along_y(1))
        send(gbuf.at[1, rows], gbuf.at[2, rows], g_s.at[at + 5], g_r.at[at + 5], along_y(3))

    def gathered(chunk):
        at = chunk * 6
        arrived(gbuf.at[3, half_rows(chunk, 1)], g_s.at[at + 1], g_r.at[at + 1], along_y(3))
        arrived(gbuf.at[1, half_rows(chunk, 0)], g_s.at[at + 2], g_r.at[at + 2], along_y(1))
        arrived(gbuf.at[2, half_rows(chunk, 0)], g_s.at[at + 4], g_r.at[at + 4], along_y(3))
        arrived(gbuf.at[2, half_rows(chunk, 1)], g_s.at[at + 5], g_r.at[at + 5], along_y(1))

    stores = []

    def project(chunk):
        rows = pl.ds(chunk_rows[chunk], BLOCK)

        def one_tile(n, carry):
            cols = pl.ds(pl.multiple_of(n * 256, 256), 256)
            total = jnp.zeros((BLOCK, 256), F32)
            for j in range(GROUP):
                total += jnp.dot(gbuf[j, rows], wbuf[j, :, cols], preferred_element_type=F32)
            obuf[rows, cols] = total.astype(BF16)
            return carry

        lax.fori_loop(0, COLS // 256, one_tile, 0)
        copy = pltpu.make_async_copy(obuf.at[rows], out_hbm.at[rows], store_sem.at[chunk])
        copy.start()
        stores.append(copy)

    finish(512)
    share(0)
    finish(768)
    share(1)
    band_arrived()
    attend(0, 0)
    relay(0)
    finish(0)
    share(2)
    attend(0, 1)
    finish(256)
    share(3)
    relay(1)

    for d in range(1, GROUP):
        rows = piece_rows(d, core)
        arrived(wbuf.at[foreign, rows], wx_s.at[d], wx_r.at[d], along_x(GROUP - d))
        send(wbuf.at[foreign, rows], wbuf.at[foreign, rows], wc_s.at[d], wc_r.at[d], partner)
    for d in range(GROUP):
        arrived(wbuf.at[foreign, piece_rows(d, 1 - core)], wc_s.at[d], wc_r.at[d], partner)
    loads[3].wait()

    gathered(0)
    project(0)
    relay(2)
    gathered(1)
    project(1)
    relay(3)
    gathered(2)
    project(2)
    gathered(3)
    project(3)
    for copy in stores:
        copy.wait()
    for copy in sent:
        copy.wait_send()


def body(queries, keys, values, span_bounds, mem_decay, mem_gate, out_weight):
    smem = pl.BlockSpec(memory_space=pltpu.SMEM)
    anywhere = pl.BlockSpec(memory_space=pl.ANY)
    dma = pltpu.SemaphoreType.DMA
    return pl.pallas_call(
        kernel,
        out_shape=jax.ShapeDtypeStruct((SEG, COLS), BF16),
        in_specs=[smem, smem, smem, anywhere, anywhere, anywhere, anywhere],
        out_specs=anywhere,
        scratch_shapes=[
            pltpu.VMEM((BAND + SEG, HEADS * WIDTH), BF16),
            pltpu.VMEM((BAND + SEG, HEADS * WIDTH), BF16),
            pltpu.VMEM((SEG, HEADS * WIDTH), BF16),
            pltpu.VMEM((GROUP, SEG, HEADS * WIDTH), BF16),
            pltpu.VMEM((GROUP, HEADS * WIDTH, COLS), BF16),
            pltpu.VMEM((SEG, COLS), BF16),
            pltpu.VMEM((SEG, HEADS * WIDTH), F32),
            pltpu.VMEM((BLOCK, 2 * PART), F32),
            pltpu.VMEM((HEADS, 2 * WIDTH, WIDTH), BF16),
            pltpu.VMEM((HEADS, 2 * WIDTH, WIDTH), BF16),
            pltpu.VMEM((ROW, SLICE, WIDTH), F32),
            pltpu.VMEM((ROW, SLICE, WIDTH), F32),
            pltpu.VMEM((SLICE, WIDTH), F32),
            pltpu.VMEM((GROUP, SLICE, WIDTH), F32),
            pltpu.VMEM((ROW, SLICE, WIDTH), F32),
            pltpu.VMEM((ROW, SLICE, WIDTH), F32),
            dma((4,)), dma((4,)), dma((8,)), dma((8,)), dma((4,)), dma((4,)),
            dma((4,)), dma((4,)), dma((4,)), dma((4,)), dma((8,)), dma((8,)),
            dma((4,)), dma((4,)), dma((8,)), dma((8,)), dma((24,)), dma((24,)),
        ],
        compiler_params=pltpu.CompilerParams(
            collective_id=0, has_side_effects=True, vmem_limit_bytes=60 * 1024 * 1024
        ),
    )(span_bounds.T, mem_decay.T, mem_gate, queries, keys, values, out_weight)


def solution(mesh):
    return jax.shard_map(
        body,
        mesh=mesh,
        in_specs=(
            P("seq", "head"),
            P("seq", "head"),
            P("seq", "head"),
            P(),
            P(None, "head"),
            P("head"),
            P("head", None),
        ),
        out_specs=P("seq", "head"),
        check_vma=False,
    )
```

```python
import math

import jax
import jax.numpy as jnp
from jax import lax
from jax.experimental import pallas as pl
from jax.experimental.pallas import tpu as pltpu
from jax.sharding import PartitionSpec as P

SEG = 1024
BAND = 512
PART = 512
BLOCK = 256
HALF = 128
HEADS = 4
WIDTH = 128
COLS = 1024
GROUP = 4
ROW = 8
SLICE = 72
MESH = pl.DeviceIdType.MESH
EXPONENT = math.log2(math.e) / math.sqrt(WIDTH)
F32 = jnp.float32
BF16 = jnp.bfloat16


def feature_map(values_in):
    return jnp.where(values_in > 0, values_in + 1.0, jnp.exp(jnp.minimum(values_in, 0.0)))


def two_terms(values_in):
    high = values_in.astype(BF16)
    return high, (values_in - high.astype(F32)).astype(BF16)


def dot_last(a, b):
    return lax.dot_general(a, b, (((1,), (1,)), ((), ())), preferred_element_type=F32)


def dot_first(a, b):
    return lax.dot_general(a, b, (((0,), (0,)), ((), ())), preferred_element_type=F32)


def head_columns(head):
    return pl.ds(pl.multiple_of(head * WIDTH, WIDTH), WIDTH)


def kernel(
    spans, decay, gate, q_hbm, k_hbm, v_hbm, w_hbm, out_hbm,
    kbuf, vbuf, qbuf, gbuf, wbuf, obuf, local, bias, mem,
    slices_out, slices_in, total_out, totals_in, mem_out, mem_in,
    load_sem, store_sem, band_s, band_r, wy_s, wy_r, wx_s, wx_r, wc_s, wc_r,
    a_s, a_r, b_s, b_r, c_s, c_r, g_s, g_r,
):
    seq = lax.axis_index("seq")
    head = lax.axis_index("head")
    x, place = seq // ROW, seq % ROW
    core, z = seq % 2, (seq % ROW) // 2
    n_seq = GROUP * ROW

    def along_y(d):
        return (seq, (head + d) % GROUP)

    def along_x(d):
        return (((x + d) % GROUP) * ROW + place, head)

    def along_row(d):
        return (x * ROW + (place + d) % ROW, head)

    partner = (seq + 1 - 2 * core, head)
    following, previous = ((seq + 1) % n_seq, head), ((seq + n_seq - 1) % n_seq, head)
    sent = []

    def remote(src, dst, send_sem, recv_sem, device):
        return pltpu.make_async_remote_copy(
            src_ref=src, dst_ref=dst, send_sem=send_sem, recv_sem=recv_sem,
            device_id=device, device_id_type=MESH,
        )

    def send(src, dst, send_sem, recv_sem, device):
        copy = remote(src, dst, send_sem, recv_sem, device)
        copy.start()
        sent.append(copy)

    def arrived(dst, send_sem, recv_sem, device):
        remote(dst, dst, send_sem, recv_sem, device).wait_recv()

    loads = [
        pltpu.make_async_copy(k_hbm, kbuf.at[pl.ds(BAND, SEG)], load_sem.at[0]),
        pltpu.make_async_copy(v_hbm, vbuf.at[pl.ds(BAND, SEG)], load_sem.at[1]),
        pltpu.make_async_copy(q_hbm, qbuf, load_sem.at[2]),
        pltpu.make_async_copy(
            w_hbm.at[:, pl.ds(pl.multiple_of(head * COLS, COLS), COLS)], wbuf.at[0], load_sem.at[3]
        ),
    ]
    loads[0].start()
    loads[1].start()

    barrier = pltpu.get_barrier_semaphore()
    sources = [along_y(d) for d in range(1, GROUP)] + [along_x(d) for d in range(1, GROUP)]
    sources += [along_row(d) for d in range(1, ROW)] + [previous]
    for device in sources:
        pl.semaphore_signal(barrier, inc=1, device_id=device, device_id_type=MESH)

    def piece_rows(d, of_core):
        return pl.ds(pl.multiple_of((((x + GROUP - d) % GROUP) * 2 + of_core) * 64, 64), 64)

    own_rows = piece_rows(0, core)

    def band_piece(n):
        hbm, ref = (k_hbm, kbuf) if n % 2 == 0 else (v_hbm, vbuf)
        rows = BLOCK - (n // 2) * BLOCK
        return hbm.at[pl.ds(SEG - BAND + rows, BLOCK)], ref.at[pl.ds(rows, BLOCK)]

    def band_arrived(half):
        for n in (2 * half, 2 * half + 1):
            arrived(band_piece(n)[1], band_s.at[n], band_r.at[n], previous)

    loads[0].wait()
    loads[1].wait()
    loads[2].start()
    loads[3].start()

    def state_of(h, carry):
        cols = head_columns(h)
        total = jnp.zeros((WIDTH, 2 * WIDTH), F32)
        sums = jnp.zeros((8, WIDTH), F32)
        for t in range(SEG // BLOCK):
            rows = pl.ds(BAND + t * BLOCK, BLOCK)
            feats = feature_map(kbuf[rows, cols].astype(F32))
            total += dot_first(vbuf[rows, cols], jnp.concatenate(two_terms(feats), axis=1))
            sums += jnp.sum(feats.reshape(BLOCK // 8, 8, WIDTH), axis=0)
        state = total[:, :WIDTH] + total[:, WIDTH:]
        sums = jnp.broadcast_to(jnp.sum(sums, axis=0, keepdims=True), (8, WIDTH)).astype(BF16)
        for half in range(2):
            slices_out[2 * h + half, :64] = state[64 * half : 64 * half + 64].astype(BF16)
            slices_out[2 * h + half, 64:] = sums
        return carry

    lax.fori_loop(0, HEADS, state_of, 0)

    pl.semaphore_wait(barrier, len(sources))
    for d in range(1, ROW):
        send(
            slices_out.at[(place + d) % ROW], slices_in.at[place], a_s.at[d], a_r.at[d], along_row(d)
        )
    slices_in[place] = slices_out[place]
    for d in range(1, GROUP):
        send(
            w_hbm.at[own_rows, pl.ds(pl.multiple_of(((head + d) % GROUP) * COLS, COLS), COLS)],
            wbuf.at[GROUP - d, own_rows], wy_s.at[d], wy_r.at[d], along_y(d),
        )
    loads[2].wait()

    def attend(part, sub):
        row = part * PART + sub * BLOCK
        count = 2 * PART - sub * BLOCK
        first = spans[0, 2 * seq + part] - seq * SEG
        last = spans[1, 2 * seq + part] - seq * SEG
        r = lax.broadcasted_iota(jnp.int32, (BLOCK, count), 0)
        j = lax.broadcasted_iota(jnp.int32, (BLOCK, count), 1)
        near = (j <= r + BAND) & (j > r)
        key_at, query_at = j + (row - BAND), r + row
        if part == 0:
            near = near & (key_at >= jnp.where(seq > 0, -BAND, 0))
        same = (query_at >= first) & (query_at < last) & (key_at >= first) & (key_at < last)
        bias[:, :count] = jnp.where(near | same, 0.0, -1e30)

        def one_head(h, carry):
            cols = head_columns(h)
            keys = kbuf[pl.ds(row, count), cols]
            scores = dot_last(qbuf[pl.ds(row, BLOCK), cols], keys) + bias[:, :count]
            weights = jnp.exp2((scores - jnp.max(scores, axis=1, keepdims=True)) * EXPONENT)
            mixed = jnp.dot(
                weights.astype(BF16), vbuf[pl.ds(row, count), cols], preferred_element_type=F32
            )
            local[pl.ds(row, BLOCK), cols] = mixed / jnp.sum(weights, axis=1, keepdims=True)
            return carry

        lax.fori_loop(0, HEADS, one_head, 0)

    attend(1, 0)

    for d in range(1, ROW):
        arrived(slices_in.at[(place + ROW - d) % ROW], a_s.at[d], a_r.at[d], along_row(ROW - d))
    total = slices_in[0].astype(F32)
    for t in range(1, ROW):
        total = decay[z, x * ROW + t] * total + slices_in[t].astype(F32)
    total_out[...] = total.astype(BF16)
    for d in range(1, GROUP):
        send(total_out, totals_in.at[x], b_s.at[d], b_r.at[d], along_x(d))
    totals_in[x] = total_out[...]

    attend(1, 1)

    for d in range(1, GROUP):
        arrived(totals_in.at[(x + GROUP - d) % GROUP], b_s.at[d], b_r.at[d], along_x(GROUP - d))
    memory = jnp.zeros((SLICE, WIDTH), F32)
    for n in range(GROUP):
        product = decay[z, n * ROW]
        for t in range(1, ROW):
            product = product * decay[z, n * ROW + t]
        memory = jnp.where(n < x, product * memory + totals_in[n].astype(F32), memory)
    for t in range(ROW):
        mem_out[t] = memory.astype(BF16)
        memory = decay[z, x * ROW + t] * memory + slices_in[t].astype(F32)
    for d in range(1, ROW):
        send(mem_out.at[(place + d) % ROW], mem_in.at[place], c_s.at[d], c_r.at[d], along_row(d))
    mem_in[place] = mem_out[place]
    foreign = pl.ds(1, GROUP - 1)
    for d in range(1, GROUP):
        arrived(wbuf.at[GROUP - d, own_rows], wy_s.at[d], wy_r.at[d], along_y(GROUP - d))

    def pass_weights(d, half, at, device):
        piece = weight_half(d, half)
        send(piece, piece, wx_s.at[at], wx_r.at[at], device)

    def weight_half(d, half):
        row = (((x + GROUP - d) % GROUP) * 2 + core) * 64 + 32 * half
        return wbuf.at[foreign, pl.ds(pl.multiple_of(row, 32), 32)]

    def weights_in(d, half, at, device):
        arrived(weight_half(d, half), wx_s.at[at], wx_r.at[at], device)

    for half in (0, 1):
        pass_weights(0, half, half, along_x(1))
        pass_weights(0, 1 - half, 3 - half, along_x(3))
    send(wbuf.at[foreign, own_rows], wbuf.at[foreign, own_rows], wc_s.at[0], wc_r.at[0], partner)

    for d in range(1, ROW):
        arrived(mem_in.at[(place + ROW - d) % ROW], c_s.at[d], c_r.at[d], along_row(ROW - d))

    for n in range(4):
        send(*band_piece(n), band_s.at[n], band_r.at[n], following)

    def place_memory(h, carry):
        mem[h, :64] = mem_in[2 * h, :64]
        mem[h, 64:WIDTH] = mem_in[2 * h + 1, :64]
        mem[h, WIDTH:] = jnp.broadcast_to(mem_in[2 * h, 64:65], (WIDTH, WIDTH))
        return carry

    lax.fori_loop(0, HEADS, place_memory, 0)

    def finish(row, count):
        def one_head(h, carry):
            cols = head_columns(h)
            high, low = two_terms(feature_map(qbuf[pl.ds(row, count), cols].astype(F32)))
            both = dot_last(high, mem[h]) + dot_last(low, mem[h])
            readout = both[:, :WIDTH] / (both[:, WIDTH:] + 1.0)
            mix = 1.0 / (1.0 + jnp.exp(-jnp.full((1, WIDTH), gate[h], F32)))
            mixed = mix * readout + (1.0 - mix) * local[pl.ds(row, count), cols]
            gbuf[0, pl.ds(row, count), cols] = mixed.astype(BF16)
            return carry

        lax.fori_loop(0, HEADS, one_head, 0, unroll=True)

    chunk_rows = (512, 768, 256, 0)

    def half_rows(chunk, half):
        return pl.ds(chunk_rows[chunk] + half * HALF, HALF)

    def to_right(chunk, half):
        rows, at = half_rows(chunk, half), chunk * 6 + half
        send(gbuf.at[0, rows], gbuf.at[3, rows], g_s.at[at], g_r.at[at], along_y(1))

    def to_left(chunk, half):
        rows, at = half_rows(chunk, half), chunk * 6 + 2 + half
        send(gbuf.at[0, rows], gbuf.at[1, rows], g_s.at[at], g_r.at[at], along_y(3))

    def share(chunk):
        to_right(chunk, 0)
        to_left(chunk, 1)
        to_right(chunk, 1)
        to_left(chunk, 0)

    def relay(chunk):
        rows, at = half_rows(chunk, 0), chunk * 6
        arrived(gbuf.at[3, rows], g_s.at[at], g_r.at[at], along_y(3))
        send(gbuf.at[3, rows], gbuf.at[2, rows], g_s.at[at + 4], g_r.at[at + 4], along_y(1))
        rows = half_rows(chunk, 1)
        arrived(gbuf.at[1, rows], g_s.at[at + 3], g_r.at[at + 3], along_y(1))
        send(gbuf.at[1, rows], gbuf.at[2, rows], g_s.at[at + 5], g_r.at[at + 5], along_y(3))

    def adjacent(chunk):
        at = chunk * 6
        arrived(gbuf.at[3, half_rows(chunk, 1)], g_s.at[at + 1], g_r.at[at + 1], along_y(3))
        arrived(gbuf.at[1, half_rows(chunk, 0)], g_s.at[at + 2], g_r.at[at + 2], along_y(1))

    def opposite(chunk):
        at = chunk * 6
        arrived(gbuf.at[2, half_rows(chunk, 0)], g_s.at[at + 4], g_r.at[at + 4], along_y(3))
        arrived(gbuf.at[2, half_rows(chunk, 1)], g_s.at[at + 5], g_r.at[at + 5], along_y(1))

    stores = []

    def product(rows, cols, owners):
        total = jnp.dot(gbuf[owners[0], rows], wbuf[owners[0], :, cols], preferred_element_type=F32)
        for j in owners[1:]:
            total += jnp.dot(gbuf[j, rows], wbuf[j, :, cols], preferred_element_type=F32)
        return total

    def tiles(one_tile):
        def step(n, carry):
            one_tile(pl.ds(pl.multiple_of(n * 256, 256), 256))
            return carry

        lax.fori_loop(0, COLS // 256, step, 0)

    def store(chunk):
        rows = pl.ds(chunk_rows[chunk], BLOCK)
        copy = pltpu.make_async_copy(obuf.at[rows], out_hbm.at[rows], store_sem.at[chunk])
        copy.start()
        stores.append(copy)

    def project(chunk):
        rows = pl.ds(chunk_rows[chunk], BLOCK)

        def one_tile(cols):
            obuf[rows, cols] = product(rows, cols, (0, 1, 2, 3)).astype(BF16)

        tiles(one_tile)
        store(chunk)

    def project_near(chunk):
        rows = pl.ds(chunk_rows[chunk], BLOCK)

        def one_tile(cols):
            bias[:, cols] = product(rows, cols, (0, 1, 3))

        tiles(one_tile)

    def project_far(chunk):
        rows = pl.ds(chunk_rows[chunk], BLOCK)

        def one_tile(cols):
            obuf[rows, cols] = (bias[:, cols] + product(rows, cols, (2,))).astype(BF16)

        tiles(one_tile)
        store(chunk)

    finish(512, HALF)
    to_right(0, 0)
    to_left(0, 0)
    finish(512 + HALF, HALF)
    to_right(0, 1)
    to_left(0, 1)
    finish(768, BLOCK)
    share(1)
    weights_in(1, 0, 0, along_x(3))
    pass_weights(1, 0, 4, along_x(1))
    weights_in(3, 1, 3, along_x(1))
    pass_weights(3, 1, 5, along_x(3))
    band_arrived(0)
    attend(0, 1)
    relay(0)
    finish(256, BLOCK)
    share(2)
    relay(1)
    band_arrived(1)
    attend(0, 0)
    finish(0, BLOCK)
    share(3)

    weights_in(1, 1, 1, along_x(3))
    weights_in(3, 0, 2, along_x(1))
    weights_in(2, 0, 4, along_x(3))
    weights_in(2, 1, 5, along_x(1))
    for d in range(1, GROUP):
        rows = piece_rows(d, core)
        send(wbuf.at[foreign, rows], wbuf.at[foreign, rows], wc_s.at[d], wc_r.at[d], partner)
    for d in range(GROUP):
        arrived(wbuf.at[foreign, piece_rows(d, 1 - core)], wc_s.at[d], wc_r.at[d], partner)
    loads[3].wait()

    adjacent(0)
    opposite(0)
    project(0)
    relay(2)
    adjacent(1)
    opposite(1)
    project(1)
    relay(3)
    adjacent(2)
    opposite(2)
    project(2)
    adjacent(3)
    project_near(3)
    opposite(3)
    project_far(3)
    for copy in stores:
        copy.wait()
    for copy in sent:
        copy.wait_send()


def body(queries, keys, values, span_bounds, mem_decay, mem_gate, out_weight):
    smem = pl.BlockSpec(memory_space=pltpu.SMEM)
    anywhere = pl.BlockSpec(memory_space=pl.ANY)
    dma = pltpu.SemaphoreType.DMA
    return pl.pallas_call(
        kernel,
        out_shape=jax.ShapeDtypeStruct((SEG, COLS), BF16),
        in_specs=[smem, smem, smem, anywhere, anywhere, anywhere, anywhere],
        out_specs=anywhere,
        scratch_shapes=[
            pltpu.VMEM((BAND + SEG, HEADS * WIDTH), BF16),
            pltpu.VMEM((BAND + SEG, HEADS * WIDTH), BF16),
            pltpu.VMEM((SEG, HEADS * WIDTH), BF16),
            pltpu.VMEM((GROUP, SEG, HEADS * WIDTH), BF16),
            pltpu.VMEM((GROUP, HEADS * WIDTH, COLS), BF16),
            pltpu.VMEM((SEG, COLS), BF16),
            pltpu.VMEM((SEG, HEADS * WIDTH), F32),
            pltpu.VMEM((BLOCK, 2 * PART), F32),
            pltpu.VMEM((HEADS, 2 * WIDTH, WIDTH), BF16),
            pltpu.VMEM((ROW, SLICE, WIDTH), BF16),
            pltpu.VMEM((ROW, SLICE, WIDTH), BF16),
            pltpu.VMEM((SLICE, WIDTH), BF16),
            pltpu.VMEM((GROUP, SLICE, WIDTH), BF16),
            pltpu.VMEM((ROW, SLICE, WIDTH), BF16),
            pltpu.VMEM((ROW, SLICE, WIDTH), BF16),
            dma((4,)), dma((4,)), dma((4,)), dma((4,)), dma((4,)), dma((4,)),
            dma((6,)), dma((6,)), dma((4,)), dma((4,)), dma((8,)), dma((8,)),
            dma((4,)), dma((4,)), dma((8,)), dma((8,)), dma((24,)), dma((24,)),
        ],
        compiler_params=pltpu.CompilerParams(
            collective_id=0, has_side_effects=True, vmem_limit_bytes=60 * 1024 * 1024
        ),
    )(span_bounds.T, mem_decay.T, mem_gate, queries, keys, values, out_weight)


def solution(mesh):
    return jax.shard_map(
        body,
        mesh=mesh,
        in_specs=(
            P("seq", "head"),
            P("seq", "head"),
            P("seq", "head"),
            P(),
            P(None, "head"),
            P("head"),
            P("head", None),
        ),
        out_specs=P("seq", "head"),
        check_vma=False,
    )
```

```python
import functools
import math

import jax
import jax.numpy as jnp
from jax import lax
from jax.experimental import pallas as pl
from jax.experimental.pallas import tpu as pltpu
from jax.sharding import PartitionSpec as P

SEG = 1024
BAND = 512
PART = 512
BLOCK = 256
HALF = 128
HEADS = 4
WIDTH = 128
COLS = 1024
GROUP = 4
ROW = 8
SLICE = 72
MESH = pl.DeviceIdType.MESH
EXPONENT = math.log2(math.e) / math.sqrt(WIDTH)
F32 = jnp.float32
BF16 = jnp.bfloat16


def feature_map(values_in):
    return jnp.where(values_in > 0, values_in + 1.0, jnp.exp(jnp.minimum(values_in, 0.0)))


def two_terms(values_in):
    high = values_in.astype(BF16)
    return high, (values_in - high.astype(F32)).astype(BF16)


def dot_last(a, b):
    return lax.dot_general(a, b, (((1,), (1,)), ((), ())), preferred_element_type=F32)


def dot_first(a, b):
    return lax.dot_general(a, b, (((0,), (0,)), ((), ())), preferred_element_type=F32)


def head_columns(head):
    return pl.ds(pl.multiple_of(head * WIDTH, WIDTH), WIDTH)


def kernel(
    spans_hbm, decay_hbm, gate_hbm, q_hbm, k_hbm, v_hbm, w_hbm, out,
    spans, decay, gate, kbuf, vbuf, qbuf, gbuf, wbuf, local, bias, near_sum, mem, state_sum, key_sum,
    slices_out, slices_in, total_out, totals_in, mem_out, mem_in,
    load_sem, small_sem, send_sem, b_s, b_r, recv_sem, w_r, band_r, g_r,
):
    seq = lax.axis_index("seq")
    head = lax.axis_index("head")
    x, place = seq // ROW, seq % ROW
    core, z = seq % 2, (seq % ROW) // 2
    n_seq = GROUP * ROW

    def along_y(d):
        return (seq, (head + d) % GROUP)

    def along_x(d):
        return (((x + d) % GROUP) * ROW + place, head)

    def along_row(d):
        return (x * ROW + (place + d) % ROW, head)

    partner = (seq + 1 - 2 * core, head)
    following, previous = ((seq + 1) % n_seq, head), ((seq + n_seq - 1) % n_seq, head)
    state_sent, mem_sent, wy_sent, wx_sent, wc_sent, band_sent, g_sent = (send_sem.at[n] for n in range(7))

    def send(src, dst, send_sem, recv_sem, device):
        pltpu.make_async_remote_copy(
            src_ref=src, dst_ref=dst, send_sem=send_sem, recv_sem=recv_sem,
            device_id=device, device_id_type=MESH,
        ).start()

    def wait_bytes(like, sem):
        pltpu.make_async_copy(like, like, sem).wait()

    small = [
        pltpu.make_async_copy(src, dst, small_sem.at[n])
        for n, (src, dst) in enumerate(((spans_hbm, spans), (decay_hbm, decay), (gate_hbm, gate)))
    ]
    loads = []
    for t in range(SEG // BLOCK):
        for hbm, ref in ((k_hbm, kbuf), (v_hbm, vbuf)):
            copy = pltpu.make_async_copy(
                hbm.at[pl.ds(t * BLOCK, BLOCK)], ref.at[pl.ds(BAND + t * BLOCK, BLOCK)],
                load_sem.at[len(loads)],
            )
            copy.start()
            loads.append(copy)
    load_q = pltpu.make_async_copy(q_hbm, qbuf, load_sem.at[8])
    load_w = pltpu.make_async_copy(
        w_hbm.at[:, pl.ds(pl.multiple_of(head * COLS, COLS), COLS)], wbuf.at[0], load_sem.at[9]
    )

    barrier = pltpu.get_barrier_semaphore()
    sources = [along_y(d) for d in range(1, GROUP)] + [along_x(d) for d in range(1, GROUP)]
    sources += [along_row(d) for d in range(1, ROW)] + [previous]
    for device in sources:
        pl.semaphore_signal(barrier, inc=1, device_id=device, device_id_type=MESH)

    def piece_rows(d, of_core):
        return pl.ds(pl.multiple_of((((x + GROUP - d) % GROUP) * 2 + of_core) * 64, 64), 64)

    own_rows = piece_rows(0, core)

    def band_piece(n):
        hbm, ref = (k_hbm, kbuf) if n % 2 == 0 else (v_hbm, vbuf)
        rows = BLOCK - (n // 2) * BLOCK
        return hbm.at[pl.ds(SEG - BAND + rows, BLOCK)], ref.at[pl.ds(rows, BLOCK)]

    def band_arrived(half):
        wait_bytes(kbuf.at[pl.ds(0, 2 * BLOCK)], band_r.at[half])

    state_sum[...] = jnp.zeros((HEADS, WIDTH, 2 * WIDTH), F32)
    key_sum[...] = jnp.zeros((HEADS, 8, WIDTH), F32)
    for t in range(SEG // BLOCK):
        loads[2 * t].wait()
        loads[2 * t + 1].wait()
        rows = pl.ds(BAND + t * BLOCK, BLOCK)
        for h in range(HEADS):
            cols = pl.ds(h * WIDTH, WIDTH)
            feats = feature_map(kbuf[rows, cols].astype(F32))
            state_sum[h] += dot_first(vbuf[rows, cols], jnp.concatenate(two_terms(feats), axis=1))
            key_sum[h] += jnp.sum(feats.reshape(BLOCK // 8, 8, WIDTH), axis=0)
    load_q.start()
    load_w.start()
    for copy in small:
        copy.start()
    for h in range(HEADS):
        state = (state_sum[h, :, :WIDTH] + state_sum[h, :, WIDTH:]).astype(BF16)
        sums = jnp.sum(key_sum[h], axis=0, keepdims=True)
        for half in range(2):
            slices_out[2 * h + half, :64] = state[64 * half : 64 * half + 64]
            slices_out[2 * h + half, 64:] = jnp.broadcast_to(sums, (8, WIDTH)).astype(BF16)

    pl.semaphore_wait(barrier, len(sources))
    for d in range(1, ROW):
        send(
            slices_out.at[(place + d) % ROW], slices_in.at[place], state_sent, recv_sem.at[0], along_row(d)
        )
    slices_in[place] = slices_out[place]
    for d in range(1, GROUP):
        send(
            w_hbm.at[own_rows, pl.ds(pl.multiple_of(((head + d) % GROUP) * COLS, COLS), COLS)],
            wbuf.at[GROUP - d, own_rows], wy_sent, w_r.at[0], along_y(d),
        )
    for copy in small:
        copy.wait()
    load_q.wait()

    def attend(part, sub):
        row = part * PART + sub * BLOCK
        count = 2 * PART - sub * BLOCK
        first = spans[0, 2 * seq + part] - seq * SEG
        last = spans[1, 2 * seq + part] - seq * SEG
        r = lax.broadcasted_iota(jnp.int32, (BLOCK, count), 0)
        j = lax.broadcasted_iota(jnp.int32, (BLOCK, count), 1)
        near = (j <= r + BAND) & (j > r)
        key_at, query_at = j + (row - BAND), r + row
        if part == 0:
            near = near & (key_at >= jnp.where(seq > 0, -BAND, 0))
        same = (query_at >= first) & (query_at < last) & (key_at >= first) & (key_at < last)
        bias[:, :count] = jnp.where(near | same, 0.0, -1e30)

        def one_head(h, carry):
            cols = head_columns(h)
            keys = kbuf[pl.ds(row, count), cols]
            scores = dot_last(qbuf[pl.ds(row, BLOCK), cols], keys) + bias[:, :count]
            weights = jnp.exp2((scores - jnp.max(scores, axis=1, keepdims=True)) * EXPONENT)
            mixed = jnp.dot(
                weights.astype(BF16), vbuf[pl.ds(row, count), cols], preferred_element_type=F32
            )
            local[pl.ds(row, BLOCK), cols] = mixed / jnp.sum(weights, axis=1, keepdims=True)
            return carry

        lax.fori_loop(0, HEADS, one_head, 0)

    attend(1, 0)

    wait_bytes(slices_in.at[pl.ds(0, ROW - 1)], recv_sem.at[0])
    total = slices_in[0].astype(F32)
    for t in range(1, ROW):
        total = decay[z, x * ROW + t] * total + slices_in[t].astype(F32)
    total_out[...] = total.astype(BF16)

    def total_copy(d):
        return pltpu.make_async_remote_copy(
            src_ref=total_out, dst_ref=totals_in.at[x], send_sem=b_s.at[d], recv_sem=b_r.at[d],
            device_id=along_x(d), device_id_type=MESH,
        )

    for d in range(1, GROUP):
        pl.when(x + d < GROUP)(total_copy(d).start)

    attend(1, 1)

    for d in range(1, GROUP):
        pl.when(x >= d)(functools.partial(wait_bytes, total_out, b_r.at[d]))
    memory = jnp.zeros((SLICE, WIDTH), F32)
    for n in range(GROUP):
        product = decay[z, n * ROW]
        for t in range(1, ROW):
            product = product * decay[z, n * ROW + t]
        memory = jnp.where(n < x, product * memory + totals_in[n].astype(F32), memory)
    for t in range(ROW):
        mem_out[t] = memory.astype(BF16)
        memory = decay[z, x * ROW + t] * memory + slices_in[t].astype(F32)
    for d in range(1, ROW):
        send(mem_out.at[(place + d) % ROW], mem_in.at[place], mem_sent, recv_sem.at[1], along_row(d))
    mem_in[place] = mem_out[place]
    foreign = pl.ds(1, GROUP - 1)
    wait_bytes(wbuf.at[foreign, own_rows], w_r.at[0])

    def pass_weights(d, half, at, device):
        piece = weight_half(d, half)
        send(piece, piece, wx_sent, w_r.at[at], device)

    def weight_half(d, half):
        row = (((x + GROUP - d) % GROUP) * 2 + core) * 64 + 32 * half
        return wbuf.at[foreign, pl.ds(pl.multiple_of(row, 32), 32)]

    for half in (0, 1):
        pass_weights(0, half, (1, 3)[half], along_x(1))
        pass_weights(0, 1 - half, (2, 3)[half], along_x(3))
    send(wbuf.at[foreign, own_rows], wbuf.at[foreign, own_rows], wc_sent, w_r.at[4], partner)

    wait_bytes(mem_in.at[pl.ds(0, ROW - 1)], recv_sem.at[1])

    for n in range(4):
        send(*band_piece(n), band_sent, band_r.at[n // 2], following)

    def place_memory(h, carry):
        mem[h, :64] = mem_in[2 * h, :64]
        mem[h, 64:WIDTH] = mem_in[2 * h + 1, :64]
        mem[h, WIDTH:] = jnp.broadcast_to(mem_in[2 * h, 64:65], (WIDTH, WIDTH))
        return carry

    lax.fori_loop(0, HEADS, place_memory, 0)

    def finish(row, count):
        def one_head(h, carry):
            cols = head_columns(h)
            high, low = two_terms(feature_map(qbuf[pl.ds(row, count), cols].astype(F32)))
            both = dot_last(high, mem[h]) + dot_last(low, mem[h])
            readout = both[:, :WIDTH] / (both[:, WIDTH:] + 1.0)
            mix = 1.0 / (1.0 + jnp.exp(-jnp.full((1, WIDTH), gate[h], F32)))
            mixed = mix * readout + (1.0 - mix) * local[pl.ds(row, count), cols]
            gbuf[0, pl.ds(row, count), cols] = mixed.astype(BF16)
            return carry

        lax.fori_loop(0, HEADS, one_head, 0, unroll=True)

    chunk_rows = (512, 768, 256, 0)

    def half_rows(chunk, half):
        return pl.ds(chunk_rows[chunk] + half * HALF, HALF)

    def to_right(chunk, half):
        rows = half_rows(chunk, half)
        send(gbuf.at[0, rows], gbuf.at[3, rows], g_sent, g_r.at[chunk * 4 + (0, 2)[half]], along_y(1))

    def to_left(chunk, half):
        rows = half_rows(chunk, half)
        send(gbuf.at[0, rows], gbuf.at[1, rows], g_sent, g_r.at[chunk * 4 + (2, 1)[half]], along_y(3))

    def share(chunk):
        to_right(chunk, 0)
        to_left(chunk, 1)
        to_right(chunk, 1)
        to_left(chunk, 0)

    def relay(chunk):
        rows, at = half_rows(chunk, 0), chunk * 4
        wait_bytes(gbuf.at[3, rows], g_r.at[at])
        send(gbuf.at[3, rows], gbuf.at[2, rows], g_sent, g_r.at[at + 3], along_y(1))
        rows = half_rows(chunk, 1)
        wait_bytes(gbuf.at[1, rows], g_r.at[at + 1])
        send(gbuf.at[1, rows], gbuf.at[2, rows], g_sent, g_r.at[at + 3], along_y(3))

    def adjacent(chunk):
        wait_bytes(gbuf.at[1, pl.ds(chunk_rows[chunk], BLOCK)], g_r.at[chunk * 4 + 2])

    def opposite(chunk):
        wait_bytes(gbuf.at[2, pl.ds(chunk_rows[chunk], BLOCK)], g_r.at[chunk * 4 + 3])

    def product(rows, cols, owners):
        total = jnp.dot(gbuf[owners[0], rows], wbuf[owners[0], :, cols], preferred_element_type=F32)
        for j in owners[1:]:
            total += jnp.dot(gbuf[j, rows], wbuf[j, :, cols], preferred_element_type=F32)
        return total

    def tiles(one_tile):
        def step(n, carry):
            one_tile(pl.ds(pl.multiple_of(n * 256, 256), 256))
            return carry

        lax.fori_loop(0, COLS // 256, step, 0)

    def project(chunk):
        rows = pl.ds(chunk_rows[chunk], BLOCK)

        def one_tile(cols):
            out[rows, cols] = product(rows, cols, (0, 1, 2, 3)).astype(BF16)

        tiles(one_tile)

    def project_near(chunk, total):
        rows = pl.ds(chunk_rows[chunk], BLOCK)

        def one_tile(cols):
            total[:, cols] = product(rows, cols, (0, 1, 3))

        tiles(one_tile)

    def project_far(chunk, total):
        rows = pl.ds(chunk_rows[chunk], BLOCK)

        def one_tile(cols):
            out[rows, cols] = (total[:, cols] + product(rows, cols, (2,))).astype(BF16)

        tiles(one_tile)

    finish(512, HALF)
    to_right(0, 0)
    to_left(0, 0)
    finish(512 + HALF, HALF)
    to_right(0, 1)
    to_left(0, 1)
    finish(768, BLOCK)
    share(1)
    wait_bytes(weight_half(1, 0), w_r.at[1])
    pass_weights(1, 0, 3, along_x(1))
    wait_bytes(weight_half(3, 1), w_r.at[2])
    pass_weights(3, 1, 3, along_x(3))
    band_arrived(0)
    attend(0, 1)
    relay(0)
    finish(256, BLOCK)
    share(2)
    relay(1)
    band_arrived(1)
    attend(0, 0)
    finish(0, BLOCK)
    share(3)

    wait_bytes(wbuf.at[foreign, pl.ds(0, 128)], w_r.at[3])
    for d in range(1, GROUP):
        rows = piece_rows(d, core)
        send(wbuf.at[foreign, rows], wbuf.at[foreign, rows], wc_sent, w_r.at[4], partner)
    wait_bytes(wbuf.at[foreign, pl.ds(0, 256)], w_r.at[4])
    load_w.wait()

    adjacent(0)
    opposite(0)
    project(0)
    relay(2)
    adjacent(1)
    opposite(1)
    project(1)
    relay(3)
    adjacent(2)
    project_near(2, bias)
    adjacent(3)
    project_near(3, near_sum)
    opposite(2)
    project_far(2, bias)
    opposite(3)
    project_far(3, near_sum)
    wait_bytes(slices_in.at[pl.ds(0, ROW - 1)], state_sent)
    wait_bytes(mem_in.at[pl.ds(0, ROW - 1)], mem_sent)
    wait_bytes(wbuf.at[foreign, own_rows], wy_sent)
    wait_bytes(wbuf.at[foreign, pl.ds(0, 192)], wx_sent)
    wait_bytes(wbuf.at[foreign, pl.ds(0, 256)], wc_sent)
    wait_bytes(kbuf.at[pl.ds(0, 4 * BLOCK)], band_sent)
    wait_bytes(gbuf.at[foreign], g_sent)
    for d in range(1, GROUP):
        pl.when(x + d < GROUP)(total_copy(d).wait_send)


def body(queries, keys, values, span_bounds, mem_decay, mem_gate, out_weight):
    anywhere = pl.BlockSpec(memory_space=pl.ANY)
    dma = pltpu.SemaphoreType.DMA
    return pl.pallas_call(
        kernel,
        out_shape=pltpu.VMEM((SEG, COLS), BF16),
        in_specs=[anywhere] * 7,
        out_specs=pl.BlockSpec(memory_space=pltpu.VMEM),
        scratch_shapes=[
            pltpu.SMEM((2, 64), jnp.int32),
            pltpu.SMEM((HEADS, GROUP * ROW), F32),
            pltpu.SMEM((HEADS,), F32),
            pltpu.VMEM((BAND + SEG, HEADS * WIDTH), BF16),
            pltpu.VMEM((BAND + SEG, HEADS * WIDTH), BF16),
            pltpu.VMEM((SEG, HEADS * WIDTH), BF16),
            pltpu.VMEM((GROUP, SEG, HEADS * WIDTH), BF16),
            pltpu.VMEM((GROUP, HEADS * WIDTH, COLS), BF16),
            pltpu.VMEM((SEG, HEADS * WIDTH), F32),
            pltpu.VMEM((BLOCK, 2 * PART), F32),
            pltpu.VMEM((BLOCK, COLS), F32),
            pltpu.VMEM((HEADS, 2 * WIDTH, WIDTH), BF16),
            pltpu.VMEM((HEADS, WIDTH, 2 * WIDTH), F32),
            pltpu.VMEM((HEADS, 8, WIDTH), F32),
            pltpu.VMEM((ROW, SLICE, WIDTH), BF16),
            pltpu.VMEM((ROW, SLICE, WIDTH), BF16),
            pltpu.VMEM((SLICE, WIDTH), BF16),
            pltpu.VMEM((GROUP, SLICE, WIDTH), BF16),
            pltpu.VMEM((ROW, SLICE, WIDTH), BF16),
            pltpu.VMEM((ROW, SLICE, WIDTH), BF16),
            dma((10,)), dma((3,)), dma((7,)), dma((4,)), dma((4,)),
            dma((2,)), dma((5,)), dma((2,)), dma((16,)),
        ],
        compiler_params=pltpu.CompilerParams(
            collective_id=0, has_side_effects=True, vmem_limit_bytes=60 * 1024 * 1024
        ),
    )(span_bounds.T, mem_decay.T, mem_gate, queries, keys, values, out_weight)


def solution(mesh):
    return jax.shard_map(
        body,
        mesh=mesh,
        in_specs=(
            P("seq", "head"),
            P("seq", "head"),
            P("seq", "head"),
            P(),
            P(None, "head"),
            P("head"),
            P("head", None),
        ),
        out_specs=P("seq", "head"),
        check_vma=False,
    )
```

```python
import functools
import math

import jax
import jax.numpy as jnp
from jax import lax
from jax.experimental import pallas as pl
from jax.experimental.pallas import tpu as pltpu
from jax.sharding import PartitionSpec as P

SEG = 1024
BAND = 512
PART = 512
BLOCK = 256
HALF = 128
HEADS = 4
WIDTH = 128
COLS = 1024
GROUP = 4
ROW = 8
SLICE = 72
MESH = pl.DeviceIdType.MESH
EXPONENT = math.log2(math.e) / math.sqrt(WIDTH)
F32 = jnp.float32
BF16 = jnp.bfloat16


def feature_map(values_in):
    return jnp.where(values_in > 0, values_in + 1.0, jnp.exp(jnp.minimum(values_in, 0.0)))


def two_terms(values_in):
    high = values_in.astype(BF16)
    return high, (values_in - high.astype(F32)).astype(BF16)


def dot_last(a, b):
    return lax.dot_general(a, b, (((1,), (1,)), ((), ())), preferred_element_type=F32)


def dot_first(a, b):
    return lax.dot_general(a, b, (((0,), (0,)), ((), ())), preferred_element_type=F32)


def head_columns(head):
    return pl.ds(pl.multiple_of(head * WIDTH, WIDTH), WIDTH)


def kernel(
    spans_hbm, decay_hbm, gate_hbm, q_hbm, k_hbm, v_hbm, w_hbm, out,
    spans, decay, gate, kbuf, vbuf, qbuf, gbuf, wbuf, local, bias, near_sum, mem, state_sum, key_sum,
    slices_out, slices_in, total_out, totals_in, mem_out, mem_in, edge,
    load_sem, small_sem, send_sem, b_s, b_r, recv_sem, w_r, band_r, g_r, edge_r,
):
    seq = lax.axis_index("seq")
    head = lax.axis_index("head")
    x, place = seq // ROW, seq % ROW
    core, z = seq % 2, (seq % ROW) // 2

    def along_y(d):
        return (seq, (head + d) % GROUP)

    def along_x(d):
        return (((x + d) % GROUP) * ROW + place, head)

    def along_row(d):
        return (x * ROW + (place + d) % ROW, head)

    partner = (seq + 1 - 2 * core, head)
    state_sent, mem_sent, wy_sent, wx_sent, wc_sent, band_sent, g_sent, edge_sent = (
        send_sem.at[n] for n in range(8)
    )

    def send(src, dst, send_sem, recv_sem, device):
        pltpu.make_async_remote_copy(
            src_ref=src, dst_ref=dst, send_sem=send_sem, recv_sem=recv_sem,
            device_id=device, device_id_type=MESH,
        ).start()

    def wait_bytes(like, sem):
        pltpu.make_async_copy(like, like, sem).wait()

    small = [
        pltpu.make_async_copy(src, dst, small_sem.at[n])
        for n, (src, dst) in enumerate(((spans_hbm, spans), (decay_hbm, decay), (gate_hbm, gate)))
    ]
    for copy in small:
        copy.start()
    loads = []
    for t in range(SEG // BLOCK):
        for hbm, ref in ((k_hbm, kbuf), (v_hbm, vbuf)):
            copy = pltpu.make_async_copy(
                hbm.at[pl.ds(t * BLOCK, BLOCK)], ref.at[pl.ds(BAND + t * BLOCK, BLOCK)],
                load_sem.at[len(loads)],
            )
            copy.start()
            loads.append(copy)
    load_q = pltpu.make_async_copy(q_hbm, qbuf, load_sem.at[8])
    load_w = pltpu.make_async_copy(
        w_hbm.at[:, pl.ds(pl.multiple_of(head * COLS, COLS), COLS)], wbuf.at[0], load_sem.at[9]
    )

    barrier = pltpu.get_barrier_semaphore()
    sources = [along_y(d) for d in range(1, GROUP)] + [along_x(d) for d in range(1, GROUP)]
    sources += [along_row(d) for d in range(1, ROW)]
    for device in sources:
        pl.semaphore_signal(barrier, inc=1, device_id=device, device_id_type=MESH)

    def piece_rows(d, of_core):
        return pl.ds(pl.multiple_of((((x + GROUP - d) % GROUP) * 2 + of_core) * 64, 64), 64)

    own_rows = piece_rows(0, core)

    def band_piece(n):
        hbm, ref = (k_hbm, kbuf) if n % 2 == 0 else (v_hbm, vbuf)
        rows = BLOCK - (n // 2) * BLOCK
        return hbm.at[pl.ds(SEG - BAND + rows, BLOCK)], ref.at[pl.ds(rows, BLOCK)]

    def over_edge(pieces):
        for n in pieces:
            send(band_piece(n)[0], edge.at[n], edge_sent, edge_r.at[n], along_x(1))

    def pass_band(half):
        for n in (2 * half, 2 * half + 1):
            src, dst = band_piece(n)

            @pl.when(place == ROW - 1)
            def _():
                wait_bytes(edge.at[n], edge_r.at[n])
                send(edge.at[n], dst, band_sent, band_r.at[half], along_row(1))

            @pl.when(place < ROW - 1)
            def _():
                send(src, dst, band_sent, band_r.at[half], along_row(1))

    def band_arrived(half):
        wait_bytes(kbuf.at[pl.ds(0, 2 * BLOCK)], band_r.at[half])

    state_sum[...] = jnp.zeros((HEADS, WIDTH, 2 * WIDTH), F32)
    key_sum[...] = jnp.zeros((HEADS, 8, WIDTH), F32)
    for t in range(SEG // BLOCK):
        loads[2 * t].wait()
        loads[2 * t + 1].wait()
        if t == SEG // BLOCK - 1:
            load_q.start()
        rows = pl.ds(BAND + t * BLOCK, BLOCK)
        for h in range(HEADS):
            cols = pl.ds(h * WIDTH, WIDTH)
            feats = feature_map(kbuf[rows, cols].astype(F32))
            state_sum[h] += dot_first(vbuf[rows, cols], jnp.concatenate(two_terms(feats), axis=1))
            key_sum[h] += jnp.sum(feats.reshape(BLOCK // 8, 8, WIDTH), axis=0)
    load_w.start()
    for h in range(HEADS):
        state = (state_sum[h, :, :WIDTH] + state_sum[h, :, WIDTH:]).astype(BF16)
        sums = jnp.sum(key_sum[h], axis=0, keepdims=True)
        for half in range(2):
            slices_out[2 * h + half, :64] = state[64 * half : 64 * half + 64]
            slices_out[2 * h + half, 64:] = jnp.broadcast_to(sums, (8, WIDTH)).astype(BF16)

    pl.semaphore_wait(barrier, len(sources))
    for d in range(1, ROW):
        send(
            slices_out.at[(place + d) % ROW], slices_in.at[place], state_sent, recv_sem.at[0], along_row(d)
        )
    slices_in[place] = slices_out[place]
    for d in range(1, GROUP):
        send(
            w_hbm.at[own_rows, pl.ds(pl.multiple_of(((head + d) % GROUP) * COLS, COLS), COLS)],
            wbuf.at[GROUP - d, own_rows], wy_sent, w_r.at[0], along_y(d),
        )
    for copy in small:
        copy.wait()
    load_q.wait()

    def attend(part, sub):
        row = part * PART + sub * BLOCK
        count = 2 * PART - sub * BLOCK
        first = spans[0, 2 * seq + part] - seq * SEG
        last = spans[1, 2 * seq + part] - seq * SEG
        r = lax.broadcasted_iota(jnp.int32, (BLOCK, count), 0)
        j = lax.broadcasted_iota(jnp.int32, (BLOCK, count), 1)
        near = (j <= r + BAND) & (j > r)
        key_at, query_at = j + (row - BAND), r + row
        if part == 0:
            near = near & (key_at >= jnp.where(seq > 0, -BAND, 0))
        same = (query_at >= first) & (query_at < last) & (key_at >= first) & (key_at < last)
        bias[:, :count] = jnp.where(near | same, 0.0, -1e30)

        def one_head(h, carry):
            cols = head_columns(h)
            keys = kbuf[pl.ds(row, count), cols]
            scores = dot_last(qbuf[pl.ds(row, BLOCK), cols], keys) + bias[:, :count]
            weights = jnp.exp2((scores - jnp.max(scores, axis=1, keepdims=True)) * EXPONENT)
            mixed = jnp.dot(
                weights.astype(BF16), vbuf[pl.ds(row, count), cols], preferred_element_type=F32
            )
            local[pl.ds(row, BLOCK), cols] = mixed / jnp.sum(weights, axis=1, keepdims=True)
            return carry

        lax.fori_loop(0, HEADS, one_head, 0)

    pl.when(place == ROW - 1)(functools.partial(over_edge, (0,)))
    attend(1, 0)

    wait_bytes(slices_in.at[pl.ds(0, ROW - 1)], recv_sem.at[0])
    total = slices_in[0].astype(F32)
    for t in range(1, ROW):
        total = decay[z, x * ROW + t] * total + slices_in[t].astype(F32)
    total_out[...] = total.astype(BF16)

    def total_copy(d):
        return pltpu.make_async_remote_copy(
            src_ref=total_out, dst_ref=totals_in.at[x], send_sem=b_s.at[d], recv_sem=b_r.at[d],
            device_id=along_x(d), device_id_type=MESH,
        )

    for d in range(1, GROUP):
        pl.when(x + d < GROUP)(total_copy(d).start)

    def send_memory():
        for d in range(1, GROUP):
            pl.when(x >= d)(functools.partial(wait_bytes, total_out, b_r.at[d]))
        memory = jnp.zeros((SLICE, WIDTH), F32)
        for n in range(GROUP):
            factor = decay[z, n * ROW]
            for t in range(1, ROW):
                factor = factor * decay[z, n * ROW + t]
            memory = jnp.where(n < x, factor * memory + totals_in[n].astype(F32), memory)
        for t in range(ROW):
            mem_out[t] = memory.astype(BF16)
            memory = decay[z, x * ROW + t] * memory + slices_in[t].astype(F32)
        for d in range(1, ROW):
            send(
                mem_out.at[(place + d) % ROW], mem_in.at[place], mem_sent, recv_sem.at[1], along_row(d)
            )
        mem_in[place] = mem_out[place]

    pl.when(x == 0)(send_memory)
    attend(1, 1)
    pl.when(x > 0)(send_memory)
    pl.when(place == ROW - 1)(functools.partial(over_edge, (1, 2, 3)))
    foreign = pl.ds(1, GROUP - 1)
    def pass_weights(d, half, at, device):
        piece = weight_half(d, half)
        send(piece, piece, wx_sent, w_r.at[at], device)

    def weight_half(d, half):
        row = (((x + GROUP - d) % GROUP) * 2 + core) * 64 + 32 * half
        return wbuf.at[foreign, pl.ds(pl.multiple_of(row, 32), 32)]


    wait_bytes(mem_in.at[pl.ds(0, ROW - 1)], recv_sem.at[1])

    pass_band(0)

    def place_memory(h, carry):
        mem[h, :64] = mem_in[2 * h, :64]
        mem[h, 64:WIDTH] = mem_in[2 * h + 1, :64]
        mem[h, WIDTH:] = jnp.broadcast_to(mem_in[2 * h, 64:65], (WIDTH, WIDTH))
        return carry

    lax.fori_loop(0, HEADS, place_memory, 0)

    def finish(row, count):
        def one_head(h, carry):
            cols = head_columns(h)
            high, low = two_terms(feature_map(qbuf[pl.ds(row, count), cols].astype(F32)))
            both = dot_last(high, mem[h]) + dot_last(low, mem[h])
            readout = both[:, :WIDTH] / (both[:, WIDTH:] + 1.0)
            mix = 1.0 / (1.0 + jnp.exp(-jnp.full((1, WIDTH), gate[h], F32)))
            mixed = mix * readout + (1.0 - mix) * local[pl.ds(row, count), cols]
            gbuf[0, pl.ds(row, count), cols] = mixed.astype(BF16)
            return carry

        lax.fori_loop(0, HEADS, one_head, 0, unroll=True)

    chunk_rows = (512, 768, 256, 0)

    def half_rows(chunk, half):
        return pl.ds(chunk_rows[chunk] + half * HALF, HALF)

    def to_right(chunk, half):
        rows = half_rows(chunk, half)
        send(gbuf.at[0, rows], gbuf.at[3, rows], g_sent, g_r.at[chunk * 4 + (0, 2)[half]], along_y(1))

    def to_left(chunk, half):
        rows = half_rows(chunk, half)
        send(gbuf.at[0, rows], gbuf.at[1, rows], g_sent, g_r.at[chunk * 4 + (2, 1)[half]], along_y(3))

    def share(chunk):
        to_right(chunk, 0)
        to_left(chunk, 1)
        to_right(chunk, 1)
        to_left(chunk, 0)

    def relay(chunk):
        rows, at = half_rows(chunk, 0), chunk * 4
        wait_bytes(gbuf.at[3, rows], g_r.at[at])
        send(gbuf.at[3, rows], gbuf.at[2, rows], g_sent, g_r.at[at + 3], along_y(1))
        rows = half_rows(chunk, 1)
        wait_bytes(gbuf.at[1, rows], g_r.at[at + 1])
        send(gbuf.at[1, rows], gbuf.at[2, rows], g_sent, g_r.at[at + 3], along_y(3))

    def adjacent(chunk):
        wait_bytes(gbuf.at[1, pl.ds(chunk_rows[chunk], BLOCK)], g_r.at[chunk * 4 + 2])

    def opposite(chunk):
        wait_bytes(gbuf.at[2, pl.ds(chunk_rows[chunk], BLOCK)], g_r.at[chunk * 4 + 3])

    def product(rows, cols, owners):
        total = jnp.dot(gbuf[owners[0], rows], wbuf[owners[0], :, cols], preferred_element_type=F32)
        for j in owners[1:]:
            total += jnp.dot(gbuf[j, rows], wbuf[j, :, cols], preferred_element_type=F32)
        return total

    def tiles(one_tile, unroll=False):
        def step(n, carry):
            one_tile(pl.ds(pl.multiple_of(n * 256, 256), 256))
            return carry

        lax.fori_loop(0, COLS // 256, step, 0, unroll=unroll)

    def project(chunk):
        rows = pl.ds(chunk_rows[chunk], BLOCK)

        def one_tile(cols):
            out[rows, cols] = product(rows, cols, (0, 1, 2, 3)).astype(BF16)

        tiles(one_tile)

    def project_near(chunk, total):
        rows = pl.ds(chunk_rows[chunk], BLOCK)

        def one_tile(cols):
            total[:, cols] = product(rows, cols, (0, 1, 3))

        tiles(one_tile)

    def project_far(chunk, total):
        rows = pl.ds(chunk_rows[chunk], BLOCK)

        def one_tile(cols):
            out[rows, cols] = (total[:, cols] + product(rows, cols, (2,))).astype(BF16)

        tiles(one_tile, unroll=True)

    finish(512, HALF)
    to_right(0, 0)
    to_left(0, 0)
    finish(512 + HALF, HALF)
    to_right(0, 1)
    to_left(0, 1)
    wait_bytes(wbuf.at[foreign, own_rows], w_r.at[0])
    for half in (0, 1):
        pass_weights(0, half, (1, 3)[half], along_x(1))
        pass_weights(0, 1 - half, (2, 3)[half], along_x(3))
    send(wbuf.at[foreign, own_rows], wbuf.at[foreign, own_rows], wc_sent, w_r.at[4], partner)
    finish(768, BLOCK)
    share(1)
    pass_band(1)
    relay(0)
    band_arrived(0)
    attend(0, 1)
    finish(256, BLOCK)
    share(2)
    wait_bytes(weight_half(1, 0), w_r.at[1])
    pass_weights(1, 0, 3, along_x(1))
    wait_bytes(weight_half(3, 1), w_r.at[2])
    pass_weights(3, 1, 3, along_x(3))
    relay(1)
    band_arrived(1)
    attend(0, 0)
    finish(0, BLOCK)
    share(3)

    wait_bytes(wbuf.at[foreign, pl.ds(0, 128)], w_r.at[3])
    for d in range(1, GROUP):
        rows = piece_rows(d, core)
        send(wbuf.at[foreign, rows], wbuf.at[foreign, rows], wc_sent, w_r.at[4], partner)
    wait_bytes(wbuf.at[foreign, pl.ds(0, 256)], w_r.at[4])
    load_w.wait()

    adjacent(0)
    opposite(0)
    project(0)
    relay(2)
    adjacent(1)
    opposite(1)
    project(1)
    relay(3)
    adjacent(2)
    project_near(2, bias)
    adjacent(3)
    project_near(3, near_sum)
    opposite(2)
    project_far(2, bias)
    opposite(3)
    project_far(3, near_sum)
    wait_bytes(slices_in.at[pl.ds(0, ROW - 1)], state_sent)
    wait_bytes(mem_in.at[pl.ds(0, ROW - 1)], mem_sent)
    wait_bytes(wbuf.at[foreign, own_rows], wy_sent)
    wait_bytes(wbuf.at[foreign, pl.ds(0, 192)], wx_sent)
    wait_bytes(wbuf.at[foreign, pl.ds(0, 256)], wc_sent)
    wait_bytes(kbuf.at[pl.ds(0, 4 * BLOCK)], band_sent)
    wait_bytes(gbuf.at[foreign], g_sent)
    for d in range(1, GROUP):
        pl.when(x + d < GROUP)(total_copy(d).wait_send)
    pl.when(place == ROW - 1)(functools.partial(wait_bytes, edge, edge_sent))


def body(queries, keys, values, span_bounds, mem_decay, mem_gate, out_weight):
    anywhere = pl.BlockSpec(memory_space=pl.ANY)
    dma = pltpu.SemaphoreType.DMA
    return pl.pallas_call(
        kernel,
        out_shape=pltpu.VMEM((SEG, COLS), BF16),
        in_specs=[anywhere] * 7,
        out_specs=pl.BlockSpec(memory_space=pltpu.VMEM),
        scratch_shapes=[
            pltpu.SMEM((2, 64), jnp.int32),
            pltpu.SMEM((HEADS, GROUP * ROW), F32),
            pltpu.SMEM((HEADS,), F32),
            pltpu.VMEM((BAND + SEG, HEADS * WIDTH), BF16),
            pltpu.VMEM((BAND + SEG, HEADS * WIDTH), BF16),
            pltpu.VMEM((SEG, HEADS * WIDTH), BF16),
            pltpu.VMEM((GROUP, SEG, HEADS * WIDTH), BF16),
            pltpu.VMEM((GROUP, HEADS * WIDTH, COLS), BF16),
            pltpu.VMEM((SEG, HEADS * WIDTH), F32),
            pltpu.VMEM((BLOCK, 2 * PART), F32),
            pltpu.VMEM((BLOCK, COLS), F32),
            pltpu.VMEM((HEADS, 2 * WIDTH, WIDTH), BF16),
            pltpu.VMEM((HEADS, WIDTH, 2 * WIDTH), F32),
            pltpu.VMEM((HEADS, 8, WIDTH), F32),
            pltpu.VMEM((ROW, SLICE, WIDTH), BF16),
            pltpu.VMEM((ROW, SLICE, WIDTH), BF16),
            pltpu.VMEM((SLICE, WIDTH), BF16),
            pltpu.VMEM((GROUP, SLICE, WIDTH), BF16),
            pltpu.VMEM((ROW, SLICE, WIDTH), BF16),
            pltpu.VMEM((ROW, SLICE, WIDTH), BF16),
            pltpu.VMEM((4, BLOCK, HEADS * WIDTH), BF16),
            dma((10,)), dma((3,)), dma((8,)), dma((4,)), dma((4,)),
            dma((2,)), dma((5,)), dma((2,)), dma((16,)), dma((4,)),
        ],
        compiler_params=pltpu.CompilerParams(
            collective_id=0, has_side_effects=True, vmem_limit_bytes=60 * 1024 * 1024
        ),
    )(span_bounds.T, mem_decay.T, mem_gate, queries, keys, values, out_weight)


def solution(mesh):
    return jax.shard_map(
        body,
        mesh=mesh,
        in_specs=(
            P("seq", "head"),
            P("seq", "head"),
            P("seq", "head"),
            P(),
            P(None, "head"),
            P("head"),
            P("head", None),
        ),
        out_specs=P("seq", "head"),
        check_vma=False,
    )
```

```python
import functools
import math

import jax
import jax.numpy as jnp
from jax import lax
from jax.experimental import pallas as pl
from jax.experimental.pallas import tpu as pltpu
from jax.sharding import PartitionSpec as P

SEG = 1024
BAND = 512
PART = 512
BLOCK = 256
PIECE = 256
HALF = 128
HEADS = 4
WIDTH = 128
COLS = 1024
GROUP = 4
ROW = 8
SLICE = 72
MESH = pl.DeviceIdType.MESH
EXPONENT = math.log2(math.e) / math.sqrt(WIDTH)
F32 = jnp.float32
BF16 = jnp.bfloat16


def feature_map(values_in):
    return jnp.where(values_in > 0, values_in + 1.0, jnp.exp(jnp.minimum(values_in, 0.0)))


def two_terms(values_in):
    high = values_in.astype(BF16)
    return high, (values_in - high.astype(F32)).astype(BF16)


def dot_last(a, b):
    return lax.dot_general(a, b, (((1,), (1,)), ((), ())), preferred_element_type=F32)


def dot_first(a, b):
    return lax.dot_general(a, b, (((0,), (0,)), ((), ())), preferred_element_type=F32)


def head_columns(head):
    return pl.ds(pl.multiple_of(head * WIDTH, WIDTH), WIDTH)


def kernel(
    spans_hbm, decay_hbm, gate_hbm, q_hbm, k_hbm, v_hbm, w_hbm, out,
    spans, decay, gate, kbuf, vbuf, qbuf, gbuf, wbuf, local, bias, near_sum, mem, state_sum, key_sum,
    slices_out, slices_in, total_out, totals_in, mem_out, mem_in, edge,
    load_sem, small_sem, send_sem, b_s, b_r, recv_sem, w_r, band_r, g_r, edge_r,
):
    seq = lax.axis_index("seq")
    head = lax.axis_index("head")
    x, place = seq // ROW, seq % ROW
    core, z = seq % 2, (seq % ROW) // 2

    def along_y(d):
        return (seq, (head + d) % GROUP)

    def along_x(d):
        return (((x + d) % GROUP) * ROW + place, head)

    def along_row(d):
        return (x * ROW + (place + d) % ROW, head)

    partner = (seq + 1 - 2 * core, head)
    state_sent, mem_sent, wy_sent, wx_sent, wc_sent, band_sent, g_sent, edge_sent = (
        send_sem.at[n] for n in range(8)
    )

    def send(src, dst, send_sem, recv_sem, device):
        pltpu.make_async_remote_copy(
            src_ref=src, dst_ref=dst, send_sem=send_sem, recv_sem=recv_sem,
            device_id=device, device_id_type=MESH,
        ).start()

    def wait_bytes(like, sem):
        pltpu.make_async_copy(like, like, sem).wait()

    small = [
        pltpu.make_async_copy(src, dst, small_sem.at[n])
        for n, (src, dst) in enumerate(((spans_hbm, spans), (decay_hbm, decay), (gate_hbm, gate)))
    ]
    for copy in small:
        copy.start()
    for t in range(SEG // PIECE):
        for hbm, ref in ((k_hbm, kbuf), (v_hbm, vbuf)):
            pltpu.make_async_copy(
                hbm.at[pl.ds(t * PIECE, PIECE)], ref.at[pl.ds(BAND + t * PIECE, PIECE)], load_sem.at[t]
            ).start()
    first_rows, later_rows = pl.ds(PART, BLOCK), (pl.ds(0, PART), pl.ds(PART + BLOCK, BLOCK))
    load_q = [
        pltpu.make_async_copy(q_hbm.at[rows], qbuf.at[rows], load_sem.at[SEG // PIECE + n])
        for n, rows in enumerate((first_rows, *later_rows))
    ]
    load_q[0].start()
    load_w = pltpu.make_async_copy(
        w_hbm.at[:, pl.ds(pl.multiple_of(head * COLS, COLS), COLS)], wbuf.at[0], load_sem.at[SEG // PIECE + 3]
    )

    barrier = pltpu.get_barrier_semaphore()
    sources = [along_y(d) for d in range(1, GROUP)] + [along_x(d) for d in range(1, GROUP)]
    sources += [along_row(d) for d in range(1, ROW)]
    for device in sources:
        pl.semaphore_signal(barrier, inc=1, device_id=device, device_id_type=MESH)

    def piece_rows(d, of_core):
        return pl.ds(pl.multiple_of((((x + GROUP - d) % GROUP) * 2 + of_core) * 64, 64), 64)

    own_rows = piece_rows(0, core)

    def band_piece(n):
        hbm, ref = (k_hbm, kbuf) if n % 2 == 0 else (v_hbm, vbuf)
        rows = BLOCK - (n // 2) * BLOCK
        return hbm.at[pl.ds(SEG - BAND + rows, BLOCK)], ref.at[pl.ds(rows, BLOCK)]

    def over_edge(pieces):
        for n in pieces:
            send(band_piece(n)[0], edge.at[n], edge_sent, edge_r.at[n], along_x(1))

    def pass_band(half):
        for n in (2 * half, 2 * half + 1):
            src, dst = band_piece(n)

            @pl.when(place == ROW - 1)
            def _():
                wait_bytes(edge.at[n], edge_r.at[n])
                send(edge.at[n], dst, band_sent, band_r.at[half], along_row(1))

            @pl.when(place < ROW - 1)
            def _():
                send(src, dst, band_sent, band_r.at[half], along_row(1))

    def band_arrived(half):
        wait_bytes(kbuf.at[pl.ds(0, 2 * BLOCK)], band_r.at[half])

    state_sum[...] = jnp.zeros((HEADS, WIDTH, 2 * WIDTH), F32)
    key_sum[...] = jnp.zeros((HEADS, 8, WIDTH), F32)
    for t in range(SEG // PIECE):
        wait_bytes(kbuf.at[pl.ds(0, 2 * PIECE)], load_sem.at[t])
        rows = pl.ds(BAND + t * PIECE, PIECE)
        for h in range(HEADS):
            cols = pl.ds(h * WIDTH, WIDTH)
            feats = feature_map(kbuf[rows, cols].astype(F32))
            state_sum[h] += dot_first(vbuf[rows, cols], jnp.concatenate(two_terms(feats), axis=1))
            key_sum[h] += jnp.sum(feats.reshape(PIECE // 8, 8, WIDTH), axis=0)
    load_w.start()
    for h in range(HEADS):
        state = (state_sum[h, :, :WIDTH] + state_sum[h, :, WIDTH:]).astype(BF16)
        sums = jnp.sum(key_sum[h], axis=0, keepdims=True)
        for half in range(2):
            slices_out[2 * h + half, :64] = state[64 * half : 64 * half + 64]
            slices_out[2 * h + half, 64:] = jnp.broadcast_to(sums, (8, WIDTH)).astype(BF16)

    pl.semaphore_wait(barrier, len(sources))
    for d in range(1, ROW):
        send(
            slices_out.at[(place + d) % ROW], slices_in.at[place], state_sent, recv_sem.at[0], along_row(d)
        )
    slices_in[place] = slices_out[place]
    for d in range(1, GROUP):
        send(
            w_hbm.at[own_rows, pl.ds(pl.multiple_of(((head + d) % GROUP) * COLS, COLS), COLS)],
            wbuf.at[GROUP - d, own_rows], wy_sent, w_r.at[0], along_y(d),
        )
    for copy in small:
        copy.wait()
    load_q[0].wait()
    load_q[1].start()
    load_q[2].start()

    def attend(part, sub, first_head=0, last_head=HEADS):
        row = part * PART + sub * BLOCK
        count = 2 * PART - sub * BLOCK
        if first_head == 0:
            first = spans[0, 2 * seq + part] - seq * SEG
            last = spans[1, 2 * seq + part] - seq * SEG
            r = lax.broadcasted_iota(jnp.int32, (BLOCK, count), 0)
            j = lax.broadcasted_iota(jnp.int32, (BLOCK, count), 1)
            near = (j <= r + BAND) & (j > r)
            key_at, query_at = j + (row - BAND), r + row
            if part == 0:
                near = near & (key_at >= jnp.where(seq > 0, -BAND, 0))
            same = (query_at >= first) & (query_at < last) & (key_at >= first) & (key_at < last)
            bias[:, :count] = jnp.where(near | same, 0.0, -1e30)

        def one_head(h, carry):
            cols = head_columns(h)
            keys = kbuf[pl.ds(row, count), cols]
            scores = dot_last(qbuf[pl.ds(row, BLOCK), cols], keys) + bias[:, :count]
            weights = jnp.exp2((scores - jnp.max(scores, axis=1, keepdims=True)) * EXPONENT)
            mixed = jnp.dot(
                weights.astype(BF16), vbuf[pl.ds(row, count), cols], preferred_element_type=F32
            )
            local[pl.ds(row, BLOCK), cols] = mixed / jnp.sum(weights, axis=1, keepdims=True)
            return carry

        lax.fori_loop(first_head, last_head, one_head, 0)

    pl.when(place == ROW - 1)(functools.partial(over_edge, (0,)))
    attend(1, 0)

    wait_bytes(slices_in.at[pl.ds(0, ROW - 1)], recv_sem.at[0])
    total = slices_in[0].astype(F32)
    for t in range(1, ROW):
        total = decay[z, x * ROW + t] * total + slices_in[t].astype(F32)
    total_out[...] = total.astype(BF16)

    def total_copy(d):
        return pltpu.make_async_remote_copy(
            src_ref=total_out, dst_ref=totals_in.at[x], send_sem=b_s.at[d], recv_sem=b_r.at[d],
            device_id=along_x(d), device_id_type=MESH,
        )

    for d in range(1, GROUP):
        pl.when(x + d < GROUP)(total_copy(d).start)

    def send_memory():
        for d in range(1, GROUP):
            pl.when(x >= d)(functools.partial(wait_bytes, total_out, b_r.at[d]))
        memory = jnp.zeros((SLICE, WIDTH), F32)
        for n in range(GROUP):
            factor = decay[z, n * ROW]
            for t in range(1, ROW):
                factor = factor * decay[z, n * ROW + t]
            memory = jnp.where(n < x, factor * memory + totals_in[n].astype(F32), memory)
        for t in range(ROW):
            mem_out[t] = memory.astype(BF16)
            memory = decay[z, x * ROW + t] * memory + slices_in[t].astype(F32)
        for n in range(ROW):
            pl.when(place != n)(functools.partial(
                send, mem_out.at[n], mem_in.at[place], mem_sent, recv_sem.at[1], (x * ROW + n, head)
            ))
        mem_in[place] = mem_out[place]

    pl.when(x == 0)(send_memory)
    for copy in load_q[1:]:
        copy.wait()
    attend(1, 1, 0, 2)
    pl.when(x > 0)(send_memory)
    pl.when(place == ROW - 1)(functools.partial(over_edge, (1, 2, 3)))
    attend(1, 1, 2, HEADS)
    foreign = pl.ds(1, GROUP - 1)
    def pass_weights(d, half, at, device):
        piece = weight_half(d, half)
        send(piece, piece, wx_sent, w_r.at[at], device)

    def weight_half(d, half):
        row = (((x + GROUP - d) % GROUP) * 2 + core) * 64 + 32 * half
        return wbuf.at[foreign, pl.ds(pl.multiple_of(row, 32), 32)]


    wait_bytes(mem_in.at[pl.ds(0, ROW - 1)], recv_sem.at[1])

    def place_memory(h, carry):
        mem[h, :64] = mem_in[2 * h, :64]
        mem[h, 64:WIDTH] = mem_in[2 * h + 1, :64]
        mem[h, WIDTH:] = jnp.broadcast_to(mem_in[2 * h, 64:65], (WIDTH, WIDTH))
        return carry

    lax.fori_loop(0, HEADS, place_memory, 0)

    def finish(row, count):
        def one_head(h, carry):
            cols = head_columns(h)
            high, low = two_terms(feature_map(qbuf[pl.ds(row, count), cols].astype(F32)))
            both = dot_last(high, mem[h]) + dot_last(low, mem[h])
            readout = both[:, :WIDTH] / (both[:, WIDTH:] + 1.0)
            mix = 1.0 / (1.0 + jnp.exp(-jnp.full((1, WIDTH), gate[h], F32)))
            mixed = mix * readout + (1.0 - mix) * local[pl.ds(row, count), cols]
            gbuf[0, pl.ds(row, count), cols] = mixed.astype(BF16)
            return carry

        lax.fori_loop(0, HEADS, one_head, 0, unroll=True)

    chunk_rows = (512, 768, 256, 0)

    def half_rows(chunk, half):
        return pl.ds(chunk_rows[chunk] + half * HALF, HALF)

    def to_right(chunk, half):
        rows = half_rows(chunk, half)
        send(gbuf.at[0, rows], gbuf.at[3, rows], g_sent, g_r.at[chunk * 4 + (0, 2)[half]], along_y(1))

    def to_left(chunk, half):
        rows = half_rows(chunk, half)
        send(gbuf.at[0, rows], gbuf.at[1, rows], g_sent, g_r.at[chunk * 4 + (2, 1)[half]], along_y(3))

    def share(chunk):
        to_right(chunk, 0)
        to_left(chunk, 1)
        to_right(chunk, 1)
        to_left(chunk, 0)

    def relay(chunk):
        rows, at = half_rows(chunk, 0), chunk * 4
        wait_bytes(gbuf.at[3, rows], g_r.at[at])
        send(gbuf.at[3, rows], gbuf.at[2, rows], g_sent, g_r.at[at + 3], along_y(1))
        rows = half_rows(chunk, 1)
        wait_bytes(gbuf.at[1, rows], g_r.at[at + 1])
        send(gbuf.at[1, rows], gbuf.at[2, rows], g_sent, g_r.at[at + 3], along_y(3))

    def adjacent(chunk):
        wait_bytes(gbuf.at[1, pl.ds(chunk_rows[chunk], BLOCK)], g_r.at[chunk * 4 + 2])

    def opposite(chunk):
        wait_bytes(gbuf.at[2, pl.ds(chunk_rows[chunk], BLOCK)], g_r.at[chunk * 4 + 3])

    def product(rows, cols, owners):
        total = jnp.dot(gbuf[owners[0], rows], wbuf[owners[0], :, cols], preferred_element_type=F32)
        for j in owners[1:]:
            total += jnp.dot(gbuf[j, rows], wbuf[j, :, cols], preferred_element_type=F32)
        return total

    def tiles(one_tile, unroll=False):
        def step(n, carry):
            one_tile(pl.ds(pl.multiple_of(n * 256, 256), 256))
            return carry

        lax.fori_loop(0, COLS // 256, step, 0, unroll=unroll)

    def project(chunk):
        rows = pl.ds(chunk_rows[chunk], BLOCK)

        def one_tile(cols):
            out[rows, cols] = product(rows, cols, (0, 1, 2, 3)).astype(BF16)

        tiles(one_tile)

    def project_near(chunk, total):
        rows = pl.ds(chunk_rows[chunk], BLOCK)

        def one_tile(cols):
            total[:, cols] = product(rows, cols, (0, 1, 3))

        tiles(one_tile)

    def project_far(chunk, total):
        rows = pl.ds(chunk_rows[chunk], BLOCK)

        def one_tile(cols):
            out[rows, cols] = (total[:, cols] + product(rows, cols, (2,))).astype(BF16)

        tiles(one_tile, unroll=True)

    finish(512, HALF)
    to_right(0, 0)
    to_left(0, 0)
    finish(512 + HALF, HALF)
    to_right(0, 1)
    to_left(0, 1)
    pass_band(0)
    wait_bytes(wbuf.at[foreign, own_rows], w_r.at[0])
    for half in (0, 1):
        pass_weights(0, half, (1, 3)[half], along_x(1))
        pass_weights(0, 1 - half, (2, 3)[half], along_x(3))
    send(wbuf.at[foreign, own_rows], wbuf.at[foreign, own_rows], wc_sent, w_r.at[4], partner)
    finish(768, BLOCK)
    share(1)
    pass_band(1)
    relay(0)
    band_arrived(0)
    attend(0, 1)
    finish(256, BLOCK)
    share(2)
    wait_bytes(weight_half(1, 0), w_r.at[1])
    pass_weights(1, 0, 3, along_x(1))
    wait_bytes(weight_half(3, 1), w_r.at[2])
    pass_weights(3, 1, 3, along_x(3))
    relay(1)
    band_arrived(1)
    attend(0, 0)
    finish(0, BLOCK)
    share(3)

    wait_bytes(wbuf.at[foreign, pl.ds(0, 128)], w_r.at[3])
    for d in range(1, GROUP):
        rows = piece_rows(d, core)
        send(wbuf.at[foreign, rows], wbuf.at[foreign, rows], wc_sent, w_r.at[4], partner)
    wait_bytes(wbuf.at[foreign, pl.ds(0, 256)], w_r.at[4])
    load_w.wait()

    adjacent(0)
    opposite(0)
    project(0)
    relay(2)
    adjacent(1)
    opposite(1)
    project(1)
    relay(3)
    adjacent(2)
    project_near(2, bias)
    adjacent(3)
    project_near(3, near_sum)
    opposite(2)
    project_far(2, bias)
    opposite(3)
    project_far(3, near_sum)
    wait_bytes(slices_in.at[pl.ds(0, ROW - 1)], state_sent)
    wait_bytes(mem_in.at[pl.ds(0, ROW - 1)], mem_sent)
    wait_bytes(wbuf.at[foreign, own_rows], wy_sent)
    wait_bytes(wbuf.at[foreign, pl.ds(0, 192)], wx_sent)
    wait_bytes(wbuf.at[foreign, pl.ds(0, 256)], wc_sent)
    wait_bytes(kbuf.at[pl.ds(0, 4 * BLOCK)], band_sent)
    wait_bytes(gbuf.at[foreign], g_sent)
    for d in range(1, GROUP):
        pl.when(x + d < GROUP)(total_copy(d).wait_send)
    pl.when(place == ROW - 1)(functools.partial(wait_bytes, edge, edge_sent))


def body(queries, keys, values, span_bounds, mem_decay, mem_gate, out_weight):
    anywhere = pl.BlockSpec(memory_space=pl.ANY)
    dma = pltpu.SemaphoreType.DMA
    return pl.pallas_call(
        kernel,
        out_shape=pltpu.VMEM((SEG, COLS), BF16),
        in_specs=[anywhere] * 7,
        out_specs=pl.BlockSpec(memory_space=pltpu.VMEM),
        scratch_shapes=[
            pltpu.SMEM((2, 64), jnp.int32),
            pltpu.SMEM((HEADS, GROUP * ROW), F32),
            pltpu.SMEM((HEADS,), F32),
            pltpu.VMEM((BAND + SEG, HEADS * WIDTH), BF16),
            pltpu.VMEM((BAND + SEG, HEADS * WIDTH), BF16),
            pltpu.VMEM((SEG, HEADS * WIDTH), BF16),
            pltpu.VMEM((GROUP, SEG, HEADS * WIDTH), BF16),
            pltpu.VMEM((GROUP, HEADS * WIDTH, COLS), BF16),
            pltpu.VMEM((SEG, HEADS * WIDTH), F32),
            pltpu.VMEM((BLOCK, 2 * PART), F32),
            pltpu.VMEM((BLOCK, COLS), F32),
            pltpu.VMEM((HEADS, 2 * WIDTH, WIDTH), BF16),
            pltpu.VMEM((HEADS, WIDTH, 2 * WIDTH), F32),
            pltpu.VMEM((HEADS, 8, WIDTH), F32),
            pltpu.VMEM((ROW, SLICE, WIDTH), BF16),
            pltpu.VMEM((ROW, SLICE, WIDTH), BF16),
            pltpu.VMEM((SLICE, WIDTH), BF16),
            pltpu.VMEM((GROUP, SLICE, WIDTH), BF16),
            pltpu.VMEM((ROW, SLICE, WIDTH), BF16),
            pltpu.VMEM((ROW, SLICE, WIDTH), BF16),
            pltpu.VMEM((4, BLOCK, HEADS * WIDTH), BF16),
            dma((8,)), dma((3,)), dma((8,)), dma((4,)), dma((4,)),
            dma((2,)), dma((5,)), dma((2,)), dma((16,)), dma((4,)),
        ],
        compiler_params=pltpu.CompilerParams(
            collective_id=0, has_side_effects=True, vmem_limit_bytes=60 * 1024 * 1024
        ),
    )(span_bounds.T, mem_decay.T, mem_gate, queries, keys, values, out_weight)


def solution(mesh):
    return jax.shard_map(
        body,
        mesh=mesh,
        in_specs=(
            P("seq", "head"),
            P("seq", "head"),
            P("seq", "head"),
            P(),
            P(None, "head"),
            P("head"),
            P("head", None),
        ),
        out_specs=P("seq", "head"),
        check_vma=False,
    )
```

```python
import functools
import math

import jax
import jax.numpy as jnp
from jax import lax
from jax.experimental import pallas as pl
from jax.experimental.pallas import tpu as pltpu
from jax.sharding import PartitionSpec as P

SEG = 1024
BAND = 512
PART = 512
BLOCK = 256
PIECE = 256
HALF = 128
HEADS = 4
WIDTH = 128
COLS = 1024
GROUP = 4
ROW = 8
SLICE = 72
MESH = pl.DeviceIdType.MESH
EXPONENT = math.log2(math.e) / math.sqrt(WIDTH)
F32 = jnp.float32
BF16 = jnp.bfloat16


def feature_map(values_in):
    return jnp.where(values_in > 0, values_in + 1.0, jnp.exp(jnp.minimum(values_in, 0.0)))


def two_terms(values_in):
    high = values_in.astype(BF16)
    return high, (values_in - high.astype(F32)).astype(BF16)


def dot_last(a, b):
    return lax.dot_general(a, b, (((1,), (1,)), ((), ())), preferred_element_type=F32)


def dot_first(a, b):
    return lax.dot_general(a, b, (((0,), (0,)), ((), ())), preferred_element_type=F32)


def head_columns(head):
    return pl.ds(pl.multiple_of(head * WIDTH, WIDTH), WIDTH)


def kernel(
    spans_hbm, decay_hbm, gate_hbm, q_hbm, k_hbm, v_hbm, w_hbm, out, near_sum, far_rows, far_weight,
    spans, decay, gate, kbuf, vbuf, qbuf, gbuf, wbuf, local, bias, mem, state_sum, key_sum,
    slices_out, slices_in, total_out, totals_in, mem_out, mem_in, edge,
    load_sem, small_sem, send_sem, b_s, b_r, recv_sem, w_r, band_r, g_r, edge_r,
):
    seq = lax.axis_index("seq")
    head = lax.axis_index("head")
    x, place = seq // ROW, seq % ROW
    core, z = seq % 2, (seq % ROW) // 2

    def along_y(d):
        return (seq, (head + d) % GROUP)

    def along_x(d):
        return (((x + d) % GROUP) * ROW + place, head)

    def along_row(d):
        return (x * ROW + (place + d) % ROW, head)

    partner = (seq + 1 - 2 * core, head)
    state_sent, mem_sent, wy_sent, wx_sent, wc_sent, band_sent, g_sent, edge_sent = (
        send_sem.at[n] for n in range(8)
    )

    def send(src, dst, send_sem, recv_sem, device):
        pltpu.make_async_remote_copy(
            src_ref=src, dst_ref=dst, send_sem=send_sem, recv_sem=recv_sem,
            device_id=device, device_id_type=MESH,
        ).start()

    def wait_bytes(like, sem):
        pltpu.make_async_copy(like, like, sem).wait()

    small = [
        pltpu.make_async_copy(src, dst, small_sem.at[n])
        for n, (src, dst) in enumerate(((spans_hbm, spans), (decay_hbm, decay), (gate_hbm, gate)))
    ]
    for copy in small:
        copy.start()
    for t in range(SEG // PIECE):
        for hbm, ref in ((k_hbm, kbuf), (v_hbm, vbuf)):
            pltpu.make_async_copy(
                hbm.at[pl.ds(t * PIECE, PIECE)], ref.at[pl.ds(BAND + t * PIECE, PIECE)], load_sem.at[t]
            ).start()
    first_rows, later_rows = pl.ds(PART, BLOCK), (pl.ds(0, PART), pl.ds(PART + BLOCK, BLOCK))
    load_q = [
        pltpu.make_async_copy(q_hbm.at[rows], qbuf.at[rows], load_sem.at[SEG // PIECE + n])
        for n, rows in enumerate((first_rows, *later_rows))
    ]
    load_q[0].start()
    load_w = pltpu.make_async_copy(
        w_hbm.at[:, pl.ds(pl.multiple_of(head * COLS, COLS), COLS)], wbuf.at[0], load_sem.at[SEG // PIECE + 3]
    )

    barrier = pltpu.get_barrier_semaphore()
    sources = [along_y(d) for d in range(1, GROUP)] + [along_x(d) for d in range(1, GROUP)]
    sources += [along_row(d) for d in range(1, ROW)]
    for device in sources:
        pl.semaphore_signal(barrier, inc=1, device_id=device, device_id_type=MESH)

    def piece_rows(d, of_core):
        return pl.ds(pl.multiple_of((((x + GROUP - d) % GROUP) * 2 + of_core) * 64, 64), 64)

    own_rows = piece_rows(0, core)

    def band_piece(n):
        hbm, ref = (k_hbm, kbuf) if n % 2 == 0 else (v_hbm, vbuf)
        rows = BLOCK - (n // 2) * BLOCK
        return hbm.at[pl.ds(SEG - BAND + rows, BLOCK)], ref.at[pl.ds(rows, BLOCK)]

    def over_edge(pieces):
        for n in pieces:
            send(band_piece(n)[0], edge.at[n], edge_sent, edge_r.at[n], along_x(1))

    def pass_band(half):
        for n in (2 * half, 2 * half + 1):
            src, dst = band_piece(n)

            @pl.when(place == ROW - 1)
            def _():
                wait_bytes(edge.at[n], edge_r.at[n])
                send(edge.at[n], dst, band_sent, band_r.at[half], along_row(1))

            @pl.when(place < ROW - 1)
            def _():
                send(src, dst, band_sent, band_r.at[half], along_row(1))

    def band_arrived(half):
        wait_bytes(kbuf.at[pl.ds(0, 2 * BLOCK)], band_r.at[half])

    state_sum[...] = jnp.zeros((HEADS, WIDTH, 2 * WIDTH), F32)
    key_sum[...] = jnp.zeros((HEADS, 8, WIDTH), F32)
    for t in range(SEG // PIECE):
        wait_bytes(kbuf.at[pl.ds(0, 2 * PIECE)], load_sem.at[t])
        rows = pl.ds(BAND + t * PIECE, PIECE)
        for h in range(HEADS):
            cols = pl.ds(h * WIDTH, WIDTH)
            feats = feature_map(kbuf[rows, cols].astype(F32))
            state_sum[h] += dot_first(vbuf[rows, cols], jnp.concatenate(two_terms(feats), axis=1))
            key_sum[h] += jnp.sum(feats.reshape(PIECE // 8, 8, WIDTH), axis=0)
    load_w.start()
    for h in range(HEADS):
        state = (state_sum[h, :, :WIDTH] + state_sum[h, :, WIDTH:]).astype(BF16)
        sums = jnp.sum(key_sum[h], axis=0, keepdims=True)
        for half in range(2):
            slices_out[2 * h + half, :64] = state[64 * half : 64 * half + 64]
            slices_out[2 * h + half, 64:] = jnp.broadcast_to(sums, (8, WIDTH)).astype(BF16)

    pl.semaphore_wait(barrier, len(sources))
    for d in range(1, ROW):
        send(
            slices_out.at[(place + d) % ROW], slices_in.at[place], state_sent, recv_sem.at[0], along_row(d)
        )
    slices_in[place] = slices_out[place]
    for d in range(1, GROUP):
        send(
            w_hbm.at[own_rows, pl.ds(pl.multiple_of(((head + d) % GROUP) * COLS, COLS), COLS)],
            wbuf.at[GROUP - d, own_rows], wy_sent, w_r.at[0], along_y(d),
        )
    for copy in small:
        copy.wait()
    load_q[0].wait()
    load_q[1].start()
    load_q[2].start()

    def attend(part, sub, first_head=0, last_head=HEADS):
        row = part * PART + sub * BLOCK
        count = 2 * PART - sub * BLOCK
        if first_head == 0:
            first = spans[0, 2 * seq + part] - seq * SEG
            last = spans[1, 2 * seq + part] - seq * SEG
            r = lax.broadcasted_iota(jnp.int32, (BLOCK, count), 0)
            j = lax.broadcasted_iota(jnp.int32, (BLOCK, count), 1)
            near = (j <= r + BAND) & (j > r)
            key_at, query_at = j + (row - BAND), r + row
            if part == 0:
                near = near & (key_at >= jnp.where(seq > 0, -BAND, 0))
            same = (query_at >= first) & (query_at < last) & (key_at >= first) & (key_at < last)
            bias[:, :count] = jnp.where(near | same, 0.0, -1e30)

        def one_head(h, carry):
            cols = head_columns(h)
            keys = kbuf[pl.ds(row, count), cols]
            scores = dot_last(qbuf[pl.ds(row, BLOCK), cols], keys) + bias[:, :count]
            weights = jnp.exp2((scores - jnp.max(scores, axis=1, keepdims=True)) * EXPONENT)
            mixed = jnp.dot(
                weights.astype(BF16), vbuf[pl.ds(row, count), cols], preferred_element_type=F32
            )
            local[pl.ds(row, BLOCK), cols] = mixed / jnp.sum(weights, axis=1, keepdims=True)
            return carry

        lax.fori_loop(first_head, last_head, one_head, 0)

    pl.when(place == ROW - 1)(functools.partial(over_edge, (0,)))
    attend(1, 0)

    wait_bytes(slices_in.at[pl.ds(0, ROW - 1)], recv_sem.at[0])
    total = slices_in[0].astype(F32)
    for t in range(1, ROW):
        total = decay[z, x * ROW + t] * total + slices_in[t].astype(F32)
    total_out[...] = total.astype(BF16)

    def total_copy(d):
        return pltpu.make_async_remote_copy(
            src_ref=total_out, dst_ref=totals_in.at[x], send_sem=b_s.at[d], recv_sem=b_r.at[d],
            device_id=along_x(d), device_id_type=MESH,
        )

    for d in range(1, GROUP):
        pl.when(x + d < GROUP)(total_copy(d).start)

    def send_memory():
        for d in range(1, GROUP):
            pl.when(x >= d)(functools.partial(wait_bytes, total_out, b_r.at[d]))
        memory = jnp.zeros((SLICE, WIDTH), F32)
        for n in range(GROUP):
            factor = decay[z, n * ROW]
            for t in range(1, ROW):
                factor = factor * decay[z, n * ROW + t]
            memory = jnp.where(n < x, factor * memory + totals_in[n].astype(F32), memory)
        for t in range(ROW):
            mem_out[t] = memory.astype(BF16)
            memory = decay[z, x * ROW + t] * memory + slices_in[t].astype(F32)
        for n in range(ROW):
            pl.when(place != n)(functools.partial(
                send, mem_out.at[n], mem_in.at[place], mem_sent, recv_sem.at[1], (x * ROW + n, head)
            ))
        mem_in[place] = mem_out[place]

    pl.when(x == 0)(send_memory)
    for copy in load_q[1:]:
        copy.wait()
    attend(1, 1, 0, 2)
    pl.when(x > 0)(send_memory)
    pl.when(place == ROW - 1)(functools.partial(over_edge, (1, 2, 3)))
    attend(1, 1, 2, HEADS)
    foreign = pl.ds(1, GROUP - 1)
    def pass_weights(d, half, at, device):
        piece = weight_half(d, half)
        send(piece, piece, wx_sent, w_r.at[at], device)

    def weight_half(d, half):
        row = (((x + GROUP - d) % GROUP) * 2 + core) * 64 + 32 * half
        return wbuf.at[foreign, pl.ds(pl.multiple_of(row, 32), 32)]


    wait_bytes(mem_in.at[pl.ds(0, ROW - 1)], recv_sem.at[1])

    def place_memory(h, carry):
        mem[h, :64] = mem_in[2 * h, :64]
        mem[h, 64:WIDTH] = mem_in[2 * h + 1, :64]
        mem[h, WIDTH:] = jnp.broadcast_to(mem_in[2 * h, 64:65], (WIDTH, WIDTH))
        return carry

    lax.fori_loop(0, HEADS, place_memory, 0)

    def finish(row, count):
        def one_head(h, carry):
            cols = head_columns(h)
            high, low = two_terms(feature_map(qbuf[pl.ds(row, count), cols].astype(F32)))
            both = dot_last(high, mem[h]) + dot_last(low, mem[h])
            readout = both[:, :WIDTH] / (both[:, WIDTH:] + 1.0)
            mix = 1.0 / (1.0 + jnp.exp(-jnp.full((1, WIDTH), gate[h], F32)))
            mixed = mix * readout + (1.0 - mix) * local[pl.ds(row, count), cols]
            gbuf[0, pl.ds(row, count), cols] = mixed.astype(BF16)
            return carry

        lax.fori_loop(0, HEADS, one_head, 0, unroll=True)

    chunk_rows = (512, 768, 256, 0)

    def half_rows(chunk, half):
        return pl.ds(chunk_rows[chunk] + half * HALF, HALF)

    def to_right(chunk, half):
        rows = half_rows(chunk, half)
        send(gbuf.at[0, rows], gbuf.at[3, rows], g_sent, g_r.at[chunk * 4 + (0, 2)[half]], along_y(1))

    def to_left(chunk, half):
        rows = half_rows(chunk, half)
        send(gbuf.at[0, rows], gbuf.at[1, rows], g_sent, g_r.at[chunk * 4 + (2, 1)[half]], along_y(3))

    def share(chunk):
        to_right(chunk, 0)
        to_left(chunk, 1)
        to_right(chunk, 1)
        to_left(chunk, 0)

    def relay(chunk):
        rows, at = half_rows(chunk, 0), chunk * 4
        wait_bytes(gbuf.at[3, rows], g_r.at[at])
        send(gbuf.at[3, rows], gbuf.at[2, rows], g_sent, g_r.at[at + 3], along_y(1))
        rows = half_rows(chunk, 1)
        wait_bytes(gbuf.at[1, rows], g_r.at[at + 1])
        send(gbuf.at[1, rows], gbuf.at[2, rows], g_sent, g_r.at[at + 3], along_y(3))

    def adjacent(chunk):
        wait_bytes(gbuf.at[1, pl.ds(chunk_rows[chunk], BLOCK)], g_r.at[chunk * 4 + 2])

    def opposite(chunk):
        wait_bytes(gbuf.at[2, pl.ds(chunk_rows[chunk], BLOCK)], g_r.at[chunk * 4 + 3])

    def product(rows, cols, owners):
        total = jnp.dot(gbuf[owners[0], rows], wbuf[owners[0], :, cols], preferred_element_type=F32)
        for j in owners[1:]:
            total += jnp.dot(gbuf[j, rows], wbuf[j, :, cols], preferred_element_type=F32)
        return total

    def tiles(one_tile, unroll=False):
        def step(n, carry):
            one_tile(pl.ds(pl.multiple_of(n * 256, 256), 256))
            return carry

        lax.fori_loop(0, COLS // 256, step, 0, unroll=unroll)

    def project(chunk):
        rows = pl.ds(chunk_rows[chunk], BLOCK)

        def one_tile(cols):
            out[rows, cols] = product(rows, cols, (0, 1, 2, 3)).astype(BF16)

        tiles(one_tile)

    def project_near(chunk, total):
        rows = pl.ds(chunk_rows[chunk], BLOCK)

        def one_tile(cols):
            total[:, cols] = product(rows, cols, (0, 1, 3))

        tiles(one_tile)

    def project_far(chunk, total):
        rows = pl.ds(chunk_rows[chunk], BLOCK)

        def one_tile(cols):
            out[rows, cols] = (total[:, cols] + product(rows, cols, (2,))).astype(BF16)

        tiles(one_tile, unroll=True)

    finish(512, HALF)
    to_right(0, 0)
    to_left(0, 0)
    finish(512 + HALF, HALF)
    to_right(0, 1)
    to_left(0, 1)
    pass_band(0)
    wait_bytes(wbuf.at[foreign, own_rows], w_r.at[0])
    for half in (0, 1):
        pass_weights(0, half, (1, 3)[half], along_x(1))
        pass_weights(0, 1 - half, (2, 3)[half], along_x(3))
    send(wbuf.at[foreign, own_rows], wbuf.at[foreign, own_rows], wc_sent, w_r.at[4], partner)
    finish(768, BLOCK)
    share(1)
    pass_band(1)
    relay(0)
    band_arrived(0)
    attend(0, 1)
    finish(256, BLOCK)
    share(2)
    wait_bytes(weight_half(1, 0), w_r.at[1])
    pass_weights(1, 0, 3, along_x(1))
    wait_bytes(weight_half(3, 1), w_r.at[2])
    pass_weights(3, 1, 3, along_x(3))
    relay(1)
    band_arrived(1)
    attend(0, 0)
    finish(0, BLOCK)
    share(3)

    wait_bytes(wbuf.at[foreign, pl.ds(0, 128)], w_r.at[3])
    for d in range(1, GROUP):
        rows = piece_rows(d, core)
        send(wbuf.at[foreign, rows], wbuf.at[foreign, rows], wc_sent, w_r.at[4], partner)
    wait_bytes(wbuf.at[foreign, pl.ds(0, 256)], w_r.at[4])
    load_w.wait()
    keep_w = pltpu.make_async_copy(wbuf.at[2], far_weight, load_sem.at[0])
    keep_w.start()

    adjacent(0)
    opposite(0)
    project(0)
    relay(2)
    adjacent(1)
    opposite(1)
    project(1)
    relay(3)
    adjacent(2)
    project_near(2, bias)
    adjacent(3)
    project_near(3, near_sum)
    opposite(2)
    project_far(2, bias)
    keep_w.wait()
    opposite(3)
    far_rows[...] = gbuf[2, :BLOCK]
    wait_bytes(slices_in.at[pl.ds(0, ROW - 1)], state_sent)
    wait_bytes(mem_in.at[pl.ds(0, ROW - 1)], mem_sent)
    wait_bytes(wbuf.at[foreign, own_rows], wy_sent)
    wait_bytes(wbuf.at[foreign, pl.ds(0, 192)], wx_sent)
    wait_bytes(wbuf.at[foreign, pl.ds(0, 256)], wc_sent)
    wait_bytes(kbuf.at[pl.ds(0, 4 * BLOCK)], band_sent)
    wait_bytes(gbuf.at[foreign], g_sent)
    for d in range(1, GROUP):
        pl.when(x + d < GROUP)(total_copy(d).wait_send)
    pl.when(place == ROW - 1)(functools.partial(wait_bytes, edge, edge_sent))


def write_out(mixed, near_sum, far_rows, far_weight, out, last, sems):
    rest = pl.ds(BLOCK, SEG - BLOCK)
    copy = pltpu.make_async_copy(mixed.at[rest], out.at[rest], sems.at[0])
    copy.start()
    for n in range(COLS // 256):
        cols = pl.ds(n * 256, 256)
        far = jnp.dot(far_rows[...], far_weight[:, cols], preferred_element_type=F32)
        last[:, cols] = (near_sum[:, cols] + far).astype(BF16)
    tail = pltpu.make_async_copy(last, out.at[pl.ds(0, BLOCK)], sems.at[1])
    tail.start()
    copy.wait()
    tail.wait()


def body(queries, keys, values, span_bounds, mem_decay, mem_gate, out_weight):
    anywhere = pl.BlockSpec(memory_space=pl.ANY)
    dma = pltpu.SemaphoreType.DMA
    operands = (span_bounds.T, mem_decay.T, mem_gate, queries, keys, values, out_weight)
    parts = pl.pallas_call(
        kernel,
        out_shape=(
            pltpu.VMEM((SEG, COLS), BF16), pltpu.VMEM((BLOCK, COLS), F32),
            pltpu.VMEM((BLOCK, HEADS * WIDTH), BF16), pltpu.VMEM((HEADS * WIDTH, COLS), BF16),
        ),
        in_specs=[anywhere] * 7,
        out_specs=[pl.BlockSpec(memory_space=pltpu.VMEM)] * 4,
        scratch_shapes=[
            pltpu.SMEM((2, 64), jnp.int32),
            pltpu.SMEM((HEADS, GROUP * ROW), F32),
            pltpu.SMEM((HEADS,), F32),
            pltpu.VMEM((BAND + SEG, HEADS * WIDTH), BF16),
            pltpu.VMEM((BAND + SEG, HEADS * WIDTH), BF16),
            pltpu.VMEM((SEG, HEADS * WIDTH), BF16),
            pltpu.VMEM((GROUP, SEG, HEADS * WIDTH), BF16),
            pltpu.VMEM((GROUP, HEADS * WIDTH, COLS), BF16),
            pltpu.VMEM((SEG, HEADS * WIDTH), F32),
            pltpu.VMEM((BLOCK, 2 * PART), F32),
            pltpu.VMEM((HEADS, 2 * WIDTH, WIDTH), BF16),
            pltpu.VMEM((HEADS, WIDTH, 2 * WIDTH), F32),
            pltpu.VMEM((HEADS, 8, WIDTH), F32),
            pltpu.VMEM((ROW, SLICE, WIDTH), BF16),
            pltpu.VMEM((ROW, SLICE, WIDTH), BF16),
            pltpu.VMEM((SLICE, WIDTH), BF16),
            pltpu.VMEM((GROUP, SLICE, WIDTH), BF16),
            pltpu.VMEM((ROW, SLICE, WIDTH), BF16),
            pltpu.VMEM((ROW, SLICE, WIDTH), BF16),
            pltpu.VMEM((4, BLOCK, HEADS * WIDTH), BF16),
            dma((8,)), dma((3,)), dma((8,)), dma((4,)), dma((4,)),
            dma((2,)), dma((5,)), dma((2,)), dma((16,)), dma((4,)),
        ],
        compiler_params=pltpu.CompilerParams(
            collective_id=0, has_side_effects=True, vmem_limit_bytes=52 * 1024 * 1024
        ),
    )(*(pltpu.with_memory_space_constraint(a, pltpu.HBM) for a in operands))
    return pl.pallas_call(
        write_out,
        out_shape=jax.ShapeDtypeStruct((SEG, COLS), BF16),
        in_specs=[anywhere] + [pl.BlockSpec(memory_space=pltpu.VMEM)] * 3,
        out_specs=anywhere,
        scratch_shapes=[pltpu.VMEM((BLOCK, COLS), BF16), dma((2,))],
        compiler_params=pltpu.CompilerParams(vmem_limit_bytes=8 * 1024 * 1024),
    )(*parts)


def solution(mesh):
    return jax.shard_map(
        body,
        mesh=mesh,
        in_specs=(
            P("seq", "head"),
            P("seq", "head"),
            P("seq", "head"),
            P(),
            P(None, "head"),
            P("head"),
            P("head", None),
        ),
        out_specs=P("seq", "head"),
        check_vma=False,
    )
```

```python
import functools
import math

import jax
import jax.numpy as jnp
from jax import lax
from jax.experimental import pallas as pl
from jax.experimental.pallas import tpu as pltpu
from jax.sharding import PartitionSpec as P

SEG = 1024
BAND = 512
PART = 512
BLOCK = 256
PIECE = 256
HALF = 128
HEADS = 4
WIDTH = 128
COLS = 1024
GROUP = 4
ROW = 8
SLICE = 72
MESH = pl.DeviceIdType.MESH
EXPONENT = math.log2(math.e) / math.sqrt(WIDTH)
F32 = jnp.float32
BF16 = jnp.bfloat16


def feature_map(values_in):
    return jnp.where(values_in > 0, values_in + 1.0, jnp.exp(jnp.minimum(values_in, 0.0)))


def two_terms(values_in):
    high = values_in.astype(BF16)
    return high, (values_in - high.astype(F32)).astype(BF16)


def dot_last(a, b):
    return lax.dot_general(a, b, (((1,), (1,)), ((), ())), preferred_element_type=F32)


def dot_first(a, b):
    return lax.dot_general(a, b, (((0,), (0,)), ((), ())), preferred_element_type=F32)


def head_columns(head):
    return pl.ds(pl.multiple_of(head * WIDTH, WIDTH), WIDTH)


def kernel(
    spans_hbm, decay_hbm, gate_hbm, q_hbm, k_hbm, v_hbm, w_hbm, out, near_sum, far_rows, far_weight,
    spans, decay, gate, kbuf, vbuf, qbuf, gbuf, wbuf, local, bias, mem, state_sum, key_sum,
    slices_out, slices_in, total_out, totals_in, mem_out, mem_in, edge, early,
    load_sem, small_sem, send_sem, b_s, b_r, recv_sem, w_r, band_r, g_r, edge_r,
):
    seq = lax.axis_index("seq")
    head = lax.axis_index("head")
    x, place = seq // ROW, seq % ROW
    core, z = seq % 2, (seq % ROW) // 2

    def along_y(d):
        return (seq, (head + d) % GROUP)

    def along_x(d):
        return (((x + d) % GROUP) * ROW + place, head)

    def along_row(d):
        return (x * ROW + (place + d) % ROW, head)

    partner = (seq + 1 - 2 * core, head)
    state_sent, mem_sent, wy_sent, wx_sent, wc_sent, band_sent, g_sent, edge_sent = (
        send_sem.at[n] for n in range(8)
    )

    def send(src, dst, send_sem, recv_sem, device):
        pltpu.make_async_remote_copy(
            src_ref=src, dst_ref=dst, send_sem=send_sem, recv_sem=recv_sem,
            device_id=device, device_id_type=MESH,
        ).start()

    def wait_bytes(like, sem):
        pltpu.make_async_copy(like, like, sem).wait()

    small = [
        pltpu.make_async_copy(src, dst, small_sem.at[n])
        for n, (src, dst) in enumerate(((spans_hbm, spans), (decay_hbm, decay), (gate_hbm, gate)))
    ]
    for copy in small:
        copy.start()
    for t in range(SEG // PIECE):
        for hbm, ref in ((k_hbm, kbuf), (v_hbm, vbuf)):
            pltpu.make_async_copy(
                hbm.at[pl.ds(t * PIECE, PIECE)], ref.at[pl.ds(BAND + t * PIECE, PIECE)], load_sem.at[t]
            ).start()
    first_rows, later_rows = pl.ds(PART, BLOCK), (pl.ds(0, PART), pl.ds(PART + BLOCK, BLOCK))
    load_q = [
        pltpu.make_async_copy(q_hbm.at[rows], qbuf.at[rows], load_sem.at[SEG // PIECE + n])
        for n, rows in enumerate((first_rows, *later_rows))
    ]
    load_q[0].start()
    load_w = pltpu.make_async_copy(
        w_hbm.at[:, pl.ds(pl.multiple_of(head * COLS, COLS), COLS)], wbuf.at[0], load_sem.at[SEG // PIECE + 3]
    )

    barrier = pltpu.get_barrier_semaphore()
    sources = [along_y(d) for d in range(1, GROUP)] + [along_x(d) for d in range(1, GROUP)]
    sources += [along_row(d) for d in range(1, ROW)]
    for device in sources:
        pl.semaphore_signal(barrier, inc=1, device_id=device, device_id_type=MESH)

    def piece_rows(d, of_core):
        return pl.ds(pl.multiple_of((((x + GROUP - d) % GROUP) * 2 + of_core) * 64, 64), 64)

    own_rows = piece_rows(0, core)

    def band_piece(n):
        hbm, ref = (k_hbm, kbuf) if n % 2 == 0 else (v_hbm, vbuf)
        rows = BLOCK - (n // 2) * BLOCK
        return hbm.at[pl.ds(SEG - BAND + rows, BLOCK)], ref.at[pl.ds(rows, BLOCK)]

    def over_edge(pieces):
        for n in pieces:
            send(band_piece(n)[0], edge.at[n], edge_sent, edge_r.at[n], along_x(1))

    def pass_band(half):
        for n in (2 * half, 2 * half + 1):
            src, dst = band_piece(n)

            @pl.when(place == ROW - 1)
            def _():
                wait_bytes(edge.at[n], edge_r.at[n])
                send(edge.at[n], dst, band_sent, band_r.at[half], along_row(1))

            @pl.when(place < ROW - 1)
            def _():
                send(src, dst, band_sent, band_r.at[half], along_row(1))

    def band_arrived(half):
        wait_bytes(kbuf.at[pl.ds(0, 2 * BLOCK)], band_r.at[half])

    state_sum[...] = jnp.zeros((HEADS, WIDTH, 2 * WIDTH), F32)
    key_sum[...] = jnp.zeros((HEADS, 8, WIDTH), F32)
    for t in range(SEG // PIECE):
        wait_bytes(kbuf.at[pl.ds(0, 2 * PIECE)], load_sem.at[t])
        rows = pl.ds(BAND + t * PIECE, PIECE)
        for h in range(HEADS):
            cols = pl.ds(h * WIDTH, WIDTH)
            feats = feature_map(kbuf[rows, cols].astype(F32))
            state_sum[h] += dot_first(vbuf[rows, cols], jnp.concatenate(two_terms(feats), axis=1))
            key_sum[h] += jnp.sum(feats.reshape(PIECE // 8, 8, WIDTH), axis=0)
    load_w.start()
    for h in range(HEADS):
        state = (state_sum[h, :, :WIDTH] + state_sum[h, :, WIDTH:]).astype(BF16)
        sums = jnp.sum(key_sum[h], axis=0, keepdims=True)
        for half in range(2):
            slices_out[2 * h + half, :64] = state[64 * half : 64 * half + 64]
            slices_out[2 * h + half, 64:] = jnp.broadcast_to(sums, (8, WIDTH)).astype(BF16)

    pl.semaphore_wait(barrier, len(sources))
    for d in range(1, ROW):
        send(
            slices_out.at[(place + d) % ROW], slices_in.at[place], state_sent, recv_sem.at[0], along_row(d)
        )
    slices_in[place] = slices_out[place]
    for d in range(1, GROUP):
        send(
            w_hbm.at[own_rows, pl.ds(pl.multiple_of(((head + d) % GROUP) * COLS, COLS), COLS)],
            wbuf.at[GROUP - d, own_rows], wy_sent, w_r.at[0], along_y(d),
        )
    for copy in small:
        copy.wait()
    load_q[0].wait()
    load_q[1].start()
    load_q[2].start()

    def attend(part, sub, first_head=0, last_head=HEADS):
        row = part * PART + sub * BLOCK
        count = 2 * PART - sub * BLOCK
        if first_head == 0:
            first = spans[0, 2 * seq + part] - seq * SEG
            last = spans[1, 2 * seq + part] - seq * SEG
            r = lax.broadcasted_iota(jnp.int32, (BLOCK, count), 0)
            j = lax.broadcasted_iota(jnp.int32, (BLOCK, count), 1)
            near = (j <= r + BAND) & (j > r)
            key_at, query_at = j + (row - BAND), r + row
            if part == 0:
                near = near & (key_at >= jnp.where(seq > 0, -BAND, 0))
            same = (query_at >= first) & (query_at < last) & (key_at >= first) & (key_at < last)
            bias[:, :count] = jnp.where(near | same, 0.0, -1e30)

        def one_head(h, carry):
            cols = head_columns(h)
            keys = kbuf[pl.ds(row, count), cols]
            scores = dot_last(qbuf[pl.ds(row, BLOCK), cols], keys) + bias[:, :count]
            weights = jnp.exp2((scores - jnp.max(scores, axis=1, keepdims=True)) * EXPONENT)
            mixed = jnp.dot(
                weights.astype(BF16), vbuf[pl.ds(row, count), cols], preferred_element_type=F32
            )
            local[pl.ds(row, BLOCK), cols] = mixed / jnp.sum(weights, axis=1, keepdims=True)
            return carry

        lax.fori_loop(first_head, last_head, one_head, 0)

    pl.when(place == ROW - 1)(functools.partial(over_edge, (0,)))
    attend(1, 0)

    wait_bytes(slices_in.at[pl.ds(0, ROW - 1)], recv_sem.at[0])
    total = slices_in[0].astype(F32)
    for t in range(1, ROW):
        total = decay[z, x * ROW + t] * total + slices_in[t].astype(F32)
    total_out[...] = total.astype(BF16)

    def total_copy(d):
        return pltpu.make_async_remote_copy(
            src_ref=total_out, dst_ref=totals_in.at[x], send_sem=b_s.at[d], recv_sem=b_r.at[d],
            device_id=along_x(d), device_id_type=MESH,
        )

    for d in range(1, GROUP):
        pl.when(x + d < GROUP)(total_copy(d).start)

    def send_memory():
        for d in range(1, GROUP):
            pl.when(x >= d)(functools.partial(wait_bytes, total_out, b_r.at[d]))
        memory = jnp.zeros((SLICE, WIDTH), F32)
        for n in range(GROUP):
            factor = decay[z, n * ROW]
            for t in range(1, ROW):
                factor = factor * decay[z, n * ROW + t]
            memory = jnp.where(n < x, factor * memory + totals_in[n].astype(F32), memory)
        for t in range(ROW):
            mem_out[t] = memory.astype(BF16)
            memory = decay[z, x * ROW + t] * memory + slices_in[t].astype(F32)
        for n in range(ROW):
            pl.when(place != n)(functools.partial(
                send, mem_out.at[n], mem_in.at[place], mem_sent, recv_sem.at[1], (x * ROW + n, head)
            ))
        mem_in[place] = mem_out[place]

    pl.when(x == 0)(send_memory)
    for copy in load_q[1:]:
        copy.wait()
    attend(1, 1, 0, 2)
    pl.when(x > 0)(send_memory)
    pl.when(place == ROW - 1)(functools.partial(over_edge, (1, 2, 3)))
    attend(1, 1, 2, HEADS)
    foreign = pl.ds(1, GROUP - 1)
    def pass_weights(d, half, at, device):
        piece = weight_half(d, half)
        send(piece, piece, wx_sent, w_r.at[at], device)

    def weight_half(d, half):
        row = (((x + GROUP - d) % GROUP) * 2 + core) * 64 + 32 * half
        return wbuf.at[foreign, pl.ds(pl.multiple_of(row, 32), 32)]


    for n, term in enumerate(two_terms(feature_map(qbuf[pl.ds(PART, HALF)].astype(F32)))):
        early[n] = term
    wait_bytes(mem_in.at[pl.ds(0, ROW - 1)], recv_sem.at[1])

    def place_memory(h, carry):
        mem[h, :64] = mem_in[2 * h, :64]
        mem[h, 64:WIDTH] = mem_in[2 * h + 1, :64]
        mem[h, WIDTH:] = jnp.broadcast_to(mem_in[2 * h, 64:65], (WIDTH, WIDTH))
        return carry

    lax.fori_loop(0, HEADS, place_memory, 0)

    def finish(row, count, ready=False):
        def one_head(h, carry):
            cols = head_columns(h)
            if ready:
                high, low = early[0, :, cols], early[1, :, cols]
            else:
                high, low = two_terms(feature_map(qbuf[pl.ds(row, count), cols].astype(F32)))
            both = dot_last(high, mem[h]) + dot_last(low, mem[h])
            readout = both[:, :WIDTH] / (both[:, WIDTH:] + 1.0)
            mix = 1.0 / (1.0 + jnp.exp(-jnp.full((1, WIDTH), gate[h], F32)))
            mixed = mix * readout + (1.0 - mix) * local[pl.ds(row, count), cols]
            gbuf[0, pl.ds(row, count), cols] = mixed.astype(BF16)
            return carry

        lax.fori_loop(0, HEADS, one_head, 0, unroll=True)

    chunk_rows = (512, 768, 256, 0)

    def half_rows(chunk, half):
        return pl.ds(chunk_rows[chunk] + half * HALF, HALF)

    def to_right(chunk, half):
        rows = half_rows(chunk, half)
        send(gbuf.at[0, rows], gbuf.at[3, rows], g_sent, g_r.at[chunk * 4 + (0, 2)[half]], along_y(1))

    def to_left(chunk, half):
        rows = half_rows(chunk, half)
        send(gbuf.at[0, rows], gbuf.at[1, rows], g_sent, g_r.at[chunk * 4 + (2, 1)[half]], along_y(3))

    def share(chunk):
        to_right(chunk, 0)
        to_left(chunk, 1)
        to_right(chunk, 1)
        to_left(chunk, 0)

    def relay(chunk):
        rows, at = half_rows(chunk, 0), chunk * 4
        wait_bytes(gbuf.at[3, rows], g_r.at[at])
        send(gbuf.at[3, rows], gbuf.at[2, rows], g_sent, g_r.at[at + 3], along_y(1))
        rows = half_rows(chunk, 1)
        wait_bytes(gbuf.at[1, rows], g_r.at[at + 1])
        send(gbuf.at[1, rows], gbuf.at[2, rows], g_sent, g_r.at[at + 3], along_y(3))

    def adjacent(chunk):
        wait_bytes(gbuf.at[1, pl.ds(chunk_rows[chunk], BLOCK)], g_r.at[chunk * 4 + 2])

    def opposite(chunk):
        wait_bytes(gbuf.at[2, pl.ds(chunk_rows[chunk], BLOCK)], g_r.at[chunk * 4 + 3])

    def product(rows, cols, owners):
        total = jnp.dot(gbuf[owners[0], rows], wbuf[owners[0], :, cols], preferred_element_type=F32)
        for j in owners[1:]:
            total += jnp.dot(gbuf[j, rows], wbuf[j, :, cols], preferred_element_type=F32)
        return total

    def tiles(one_tile, unroll=False):
        def step(n, carry):
            one_tile(pl.ds(pl.multiple_of(n * 256, 256), 256))
            return carry

        lax.fori_loop(0, COLS // 256, step, 0, unroll=unroll)

    def project(chunk):
        rows = pl.ds(chunk_rows[chunk], BLOCK)

        def one_tile(cols):
            out[rows, cols] = product(rows, cols, (0, 1, 2, 3)).astype(BF16)

        tiles(one_tile)

    def project_near(chunk, total):
        rows = pl.ds(chunk_rows[chunk], BLOCK)

        def one_tile(cols):
            total[:, cols] = product(rows, cols, (0, 1, 3))

        tiles(one_tile)

    def project_far(chunk, total):
        rows = pl.ds(chunk_rows[chunk], BLOCK)

        def one_tile(cols):
            out[rows, cols] = (total[:, cols] + product(rows, cols, (2,))).astype(BF16)

        tiles(one_tile, unroll=True)

    finish(512, HALF, ready=True)
    to_right(0, 0)
    to_left(0, 0)
    finish(512 + HALF, HALF)
    to_right(0, 1)
    to_left(0, 1)
    pass_band(0)
    wait_bytes(wbuf.at[foreign, own_rows], w_r.at[0])
    for half in (0, 1):
        pass_weights(0, half, (1, 3)[half], along_x(1))
        pass_weights(0, 1 - half, (2, 3)[half], along_x(3))
    send(wbuf.at[foreign, own_rows], wbuf.at[foreign, own_rows], wc_sent, w_r.at[4], partner)
    finish(768, BLOCK)
    share(1)
    pass_band(1)
    relay(0)
    band_arrived(0)
    attend(0, 1)
    finish(256, BLOCK)
    share(2)
    wait_bytes(weight_half(1, 0), w_r.at[1])
    pass_weights(1, 0, 3, along_x(1))
    wait_bytes(weight_half(3, 1), w_r.at[2])
    pass_weights(3, 1, 3, along_x(3))
    relay(1)
    band_arrived(1)
    attend(0, 0)
    finish(0, BLOCK)
    share(3)

    wait_bytes(wbuf.at[foreign, pl.ds(0, 128)], w_r.at[3])
    for d in range(1, GROUP):
        rows = piece_rows(d, core)
        send(wbuf.at[foreign, rows], wbuf.at[foreign, rows], wc_sent, w_r.at[4], partner)
    wait_bytes(wbuf.at[foreign, pl.ds(0, 256)], w_r.at[4])
    load_w.wait()
    keep_w = pltpu.make_async_copy(wbuf.at[2], far_weight, load_sem.at[0])
    keep_w.start()

    adjacent(0)
    opposite(0)
    project(0)
    relay(2)
    adjacent(1)
    opposite(1)
    project(1)
    relay(3)
    adjacent(2)
    project_near(2, bias)
    adjacent(3)
    project_near(3, near_sum)
    opposite(2)
    project_far(2, bias)
    keep_w.wait()
    opposite(3)
    far_rows[...] = gbuf[2, :BLOCK]
    wait_bytes(slices_in.at[pl.ds(0, ROW - 1)], state_sent)
    wait_bytes(mem_in.at[pl.ds(0, ROW - 1)], mem_sent)
    wait_bytes(wbuf.at[foreign, own_rows], wy_sent)
    wait_bytes(wbuf.at[foreign, pl.ds(0, 192)], wx_sent)
    wait_bytes(wbuf.at[foreign, pl.ds(0, 256)], wc_sent)
    wait_bytes(kbuf.at[pl.ds(0, 4 * BLOCK)], band_sent)
    wait_bytes(gbuf.at[foreign], g_sent)
    for d in range(1, GROUP):
        pl.when(x + d < GROUP)(total_copy(d).wait_send)
    pl.when(place == ROW - 1)(functools.partial(wait_bytes, edge, edge_sent))


def write_out(mixed, near_sum, far_rows, far_weight, out, last, sems):
    rest = pl.ds(BLOCK, SEG - BLOCK)
    copy = pltpu.make_async_copy(mixed.at[rest], out.at[rest], sems.at[0])
    copy.start()
    for n in range(COLS // 256):
        cols = pl.ds(n * 256, 256)
        far = jnp.dot(far_rows[...], far_weight[:, cols], preferred_element_type=F32)
        last[:, cols] = (near_sum[:, cols] + far).astype(BF16)
    tail = pltpu.make_async_copy(last, out.at[pl.ds(0, BLOCK)], sems.at[1])
    tail.start()
    copy.wait()
    tail.wait()


def body(queries, keys, values, span_bounds, mem_decay, mem_gate, out_weight):
    anywhere = pl.BlockSpec(memory_space=pl.ANY)
    dma = pltpu.SemaphoreType.DMA
    operands = (span_bounds.T, mem_decay.T, mem_gate, queries, keys, values, out_weight)
    parts = pl.pallas_call(
        kernel,
        out_shape=(
            pltpu.VMEM((SEG, COLS), BF16), pltpu.VMEM((BLOCK, COLS), F32),
            pltpu.VMEM((BLOCK, HEADS * WIDTH), BF16), pltpu.VMEM((HEADS * WIDTH, COLS), BF16),
        ),
        in_specs=[anywhere] * 7,
        out_specs=[pl.BlockSpec(memory_space=pltpu.VMEM)] * 4,
        scratch_shapes=[
            pltpu.SMEM((2, 64), jnp.int32),
            pltpu.SMEM((HEADS, GROUP * ROW), F32),
            pltpu.SMEM((HEADS,), F32),
            pltpu.VMEM((BAND + SEG, HEADS * WIDTH), BF16),
            pltpu.VMEM((BAND + SEG, HEADS * WIDTH), BF16),
            pltpu.VMEM((SEG, HEADS * WIDTH), BF16),
            pltpu.VMEM((GROUP, SEG, HEADS * WIDTH), BF16),
            pltpu.VMEM((GROUP, HEADS * WIDTH, COLS), BF16),
            pltpu.VMEM((SEG, HEADS * WIDTH), F32),
            pltpu.VMEM((BLOCK, 2 * PART), F32),
            pltpu.VMEM((HEADS, 2 * WIDTH, WIDTH), BF16),
            pltpu.VMEM((HEADS, WIDTH, 2 * WIDTH), F32),
            pltpu.VMEM((HEADS, 8, WIDTH), F32),
            pltpu.VMEM((ROW, SLICE, WIDTH), BF16),
            pltpu.VMEM((ROW, SLICE, WIDTH), BF16),
            pltpu.VMEM((SLICE, WIDTH), BF16),
            pltpu.VMEM((GROUP, SLICE, WIDTH), BF16),
            pltpu.VMEM((ROW, SLICE, WIDTH), BF16),
            pltpu.VMEM((ROW, SLICE, WIDTH), BF16),
            pltpu.VMEM((4, BLOCK, HEADS * WIDTH), BF16),
            pltpu.VMEM((2, HALF, HEADS * WIDTH), BF16),
            dma((8,)), dma((3,)), dma((8,)), dma((4,)), dma((4,)),
            dma((2,)), dma((5,)), dma((2,)), dma((16,)), dma((4,)),
        ],
        compiler_params=pltpu.CompilerParams(
            collective_id=0, has_side_effects=True, vmem_limit_bytes=52 * 1024 * 1024
        ),
    )(*(pltpu.with_memory_space_constraint(a, pltpu.HBM) for a in operands))
    return pl.pallas_call(
        write_out,
        out_shape=jax.ShapeDtypeStruct((SEG, COLS), BF16),
        in_specs=[anywhere] + [pl.BlockSpec(memory_space=pltpu.VMEM)] * 3,
        out_specs=anywhere,
        scratch_shapes=[pltpu.VMEM((BLOCK, COLS), BF16), dma((2,))],
        compiler_params=pltpu.CompilerParams(vmem_limit_bytes=8 * 1024 * 1024),
    )(*parts)


def solution(mesh):
    return jax.shard_map(
        body,
        mesh=mesh,
        in_specs=(
            P("seq", "head"),
            P("seq", "head"),
            P("seq", "head"),
            P(),
            P(None, "head"),
            P("head"),
            P("head", None),
        ),
        out_specs=P("seq", "head"),
        check_vma=False,
    )
```
